32 devices in a mesh: case: 4 (over z), gx: 2 (over y), gy: 4 (over x, core).
Axes of the slice: x: 2, y: 2, z: 4, core: 2. Of those that a mesh axis runs over, the one named last changes fastest.
Arguments:
- velocity: bfloat16 [4, 3, 32, 64, 128], P('case', None, 'gx', 'gy'), may hold values from -4 to 3
- target: bfloat16 [4, 3, 32, 64, 128], P('case', None, 'gx', 'gy'), may hold values from -3 to 3
- weight_in: bfloat16 [256, 12], replicated, may hold values from -1.75 to 1.75
- bias_in: float32 [256], replicated, may hold values from -3 to 3
- weight_mid: bfloat16 [256, 256], replicated, may hold values from -0.375 to 0.375
- bias_mid: float32 [256], replicated, may hold values from -3 to 3
- weight_out: bfloat16 [3, 256], replicated, may hold values from -0.375 to 0.375
- bias_out: float32 [3], replicated, may hold values from -3 to 3
- thrust_coef: float32 [100], replicated, may hold values from 0.5 to 1
- tile_cells: int32 [64, 128], P(('gx', 'gy')), may hold values from 0 to 32767
- tile_turbine: int32 [64], P(('gx', 'gy')), may hold values from -1 to 99, as said below
- tile_weight: float32 [64, 128], P(('gx', 'gy')), may hold values from 0.25 to 2
Outputs:
- velocity_new: bfloat16 [4, 3, 32, 64, 128], P('case', None, 'gx', 'gy')
- loss: float32 [], replicated
- step_weight_in: float32 [256, 12], replicated
- step_bias_in: float32 [256], replicated
- step_weight_mid: float32 [256, 256], replicated
- step_bias_mid: float32 [256], replicated
- step_weight_out: float32 [3, 256], replicated
- step_bias_out: float32 [3], replicated
- force_grad: bfloat16 [4, 3, 32, 64, 128], P('case', None, 'gx', 'gy')
The draws below stay inside these ranges and needn't reach their ends.
Inputs may be any that keep to these rules, and one draw needn't show every extreme that they name: `tile_turbine`: in each device's block of 8 tile rows the used rows come first and the rest hold -1; in every draw some device has all 8 rows used.
All inputs are finite; a program needn't handle non-finite values.
Results may differ from the reference program's by a relative error of at most 0.0006.
The reference program's roundings to bfloat16 on the way (of `features`, `hidden_one`, `hidden_two`, `provisional`, `delta_two` and `delta_one`) count: a program that leaves them out, or rounds other values in their place, can miss the bound.
Values may be sent and summed in bfloat16 or wider, within the bound.
No kernel may reach another device: no remote copies, remote signals or barrier semaphores. Data moves between devices by JAX's collectives and lax.ppermute only.
A program may use at most 128 MiB of HBM per device.

```python
import math
import jax
import jax.numpy as jnp
from jax import lax

CX = 16
CY = 16
NZ = 128
UNITS = 256
FEATS = 12
TURBINES = 100
TILES_DEV = 8
DISK_ROW = 128
ITERS = 20
CASES = 4
NX = 32
NY = 64
TILES = 64
N_GX = 2
N_GY = 4


def draw_tile_turbine(key, part):
    block_total = TILES // TILES_DEV
    count_key, full_key, turbine_key = jax.random.split(jax.random.fold_in(key, 17), 3)
    row_counts = jax.random.randint(count_key, (block_total,), 0, TILES_DEV + 1)
    full_block = jax.random.randint(full_key, (), 0, block_total)
    row_counts = jnp.where(jnp.arange(block_total) == full_block, TILES_DEV, row_counts)
    turbine_ids = jax.random.randint(turbine_key, (block_total, TILES_DEV), 0, TURBINES)
    live_rows = jnp.arange(TILES_DEV)[None, :] < row_counts[:, None]
    return jnp.where(live_rows, turbine_ids, -1).reshape(TILES).astype(jnp.int32)


def draw_velocity(key, part):
    noise_key = jax.random.fold_in(key, 29)
    shape = (CASES, 3, NX, NY, NZ)
    place = jnp.arange(NX, dtype=jnp.float32) / float(max(NX - 1, 1))
    noise = jnp.clip(0.5 * jax.random.normal(noise_key, shape, jnp.float32), -2.4, 2.4)
    deficit = -0.8 * place
    stream = (jnp.arange(3) == 0).astype(jnp.float32)[:, None, None, None]
    values = noise + stream * deficit[None, :, None, None]
    return values.astype(jnp.bfloat16)


def plant(values, stream_key, low, high):
    longest = values.shape.index(max(values.shape))
    spots = []
    for shift in (0, 1):
        where = [jax.random.randint(jax.random.fold_in(stream_key, axis), (), 0, length) for axis, length in enumerate(values.shape)]
        where[longest] = (where[longest] + shift) % values.shape[longest]
        spots.append(tuple(where))
    return values.at[spots[0]].set(low).at[spots[1]].set(high)


def steps_of(key, dims, pieces, low, top_value):
    loudness = 1.0
    for dim, blocks in pieces:
        draws = jax.random.uniform(jax.random.fold_in(jax.random.fold_in(key, 6), dim), (blocks,), jnp.float32, low / len(pieces), top_value / len(pieces))
        loudness = loudness * jnp.repeat(jnp.exp(draws), dims[dim] // blocks).reshape((-1,) + (1,) * (len(dims) - 1 - dim))
    return loudness


def gaussian(key, dims, scale, bound, pieces=(), kind=jnp.bfloat16):
    result = jax.random.normal(key, dims, jnp.float32) * scale
    if len(pieces) > 0:
        result = steps_of(key, dims, pieces, -0.22, 0.18) * result
    return jnp.clip(result, min=-bound, max=bound).astype(kind)


def setup_inputs(seed: int = 0) -> dict:
    arg_keys = jax.random.split(jax.random.key(seed), 13)
    velocity = draw_velocity(jax.random.fold_in(arg_keys[12], 71), 0)
    target = gaussian(arg_keys[1], (CASES, 3, NX, NY, NZ), 0.5, 3.0, ((0, 4), (2, 2), (3, 4)))
    weight_in = gaussian(arg_keys[2], (UNITS, FEATS), FEATS ** -0.5, 1.75)
    bias_in = gaussian(arg_keys[3], (UNITS,), 0.5, 3.0, (), jnp.float32)
    weight_mid = gaussian(arg_keys[4], (UNITS, UNITS), UNITS ** -0.5, 0.375)
    bias_mid = gaussian(arg_keys[5], (UNITS,), 0.5, 3.0, (), jnp.float32)
    weight_out = gaussian(arg_keys[6], (3, UNITS), UNITS ** -0.5, 0.375)
    bias_out = gaussian(arg_keys[7], (3,), 0.5, 3.0, (), jnp.float32)
    thrust_coef = jnp.clip(jax.random.uniform(arg_keys[8], (TURBINES,), jnp.float32, 0.5, 1.0), 0.5, 1.0)
    tile_cells = plant(jax.random.randint(arg_keys[9], (TILES, DISK_ROW), 0, CX * CY * NZ), jax.random.fold_in(arg_keys[9], 1), 0, (CX * CY * NZ) - 1).astype(jnp.int32)
    tile_turbine = draw_tile_turbine(jax.random.fold_in(arg_keys[12], 71), 0)
    tile_weight = jnp.clip(jnp.exp(math.log(2.0) - 2.0794415 * jax.random.uniform(arg_keys[11], (TILES, DISK_ROW), jnp.float32) ** steps_of(arg_keys[11], (TILES, DISK_ROW), ((0, 8),), -0.2, 0.2)), 0.25, 2.0)
    return {"velocity": velocity, "target": target, "weight_in": weight_in, "bias_in": bias_in, "weight_mid": weight_mid, "bias_mid": bias_mid, "weight_out": weight_out, "bias_out": bias_out, "thrust_coef": thrust_coef, "tile_cells": tile_cells, "tile_turbine": tile_turbine, "tile_weight": tile_weight}


inflow = 1.0
step_dt = 0.4
viscosity = 0.1
epsilon_rms = 1e-06

def offset_view(extended, spatial_dim, offset):
    slicers = [slice(None)] * (extended.ndim - 3)
    for position in range(3):
        length = extended.shape[extended.ndim - 3 + position]
        if position == spatial_dim:
            slicers.append(slice(1 + offset, length - 1 + offset))
        else:
            slicers.append(slice(1, length - 1))
    return extended[tuple(slicers)]

def central(extended, spatial_dim):
    return 0.5 * (offset_view(extended, spatial_dim, 1) - offset_view(extended, spatial_dim, -1))

def neighbour_sum(extended):
    summed = offset_view(extended, 0, 1) + offset_view(extended, 0, -1)
    for spatial_dim in (1, 2):
        summed = summed + offset_view(extended, spatial_dim, 1) + offset_view(extended, spatial_dim, -1)
    return summed

def pad_all(values):
    padding = [(0, 0)] * (values.ndim - 3) + [(1, 1)] * 3
    return jnp.pad(values, padding)

def contract_cells(former, latter):
    return lax.dot_general(former, latter, (((1,), (1,)), ((), ())), preferred_element_type=jnp.float32)

def to_blocks(values):
    leading = values.shape[:-3]
    lead_count = len(leading)
    shaped = values.reshape(leading + (N_GX, CX, N_GY, CY, NZ))
    order = (lead_count, lead_count + 2) + tuple(range(lead_count)) + (lead_count + 1, lead_count + 3, lead_count + 4)
    return jnp.transpose(shaped, order).reshape((N_GX * N_GY,) + leading + (CX * CY * NZ,))

def from_blocks(blocked):
    leading = blocked.shape[1:-1]
    lead_count = len(leading)
    shaped = blocked.reshape((N_GX, N_GY) + leading + (CX, CY, NZ))
    order = tuple(range(2, 2 + lead_count)) + (0, lead_count + 2, 1, lead_count + 3, lead_count + 4)
    return jnp.transpose(shaped, order).reshape(leading + (NX, NY, NZ))

def divergence_of(extended):
    return central(extended[0], 0) + central(extended[1], 1) + central(extended[2], 2)

def pressure_correction(divergence):
    source = divergence / step_dt

    def sweep(sweep_number, pressure):
        return (neighbour_sum(pad_all(pressure)) - source) / 6.0
    pressure = lax.fori_loop(0, ITERS, sweep, jnp.zeros_like(source))
    padded = pad_all(pressure)
    return step_dt * jnp.stack([central(padded, spatial_dim) for spatial_dim in range(3)])

def closure_forward(features_block, weight_in, bias_in, weight_mid, bias_mid, weight_out, bias_out):
    hidden_one = jnp.tanh(jnp.dot(weight_in, features_block, preferred_element_type=jnp.float32) + bias_in[:, None]).astype(jnp.bfloat16)
    hidden_two = jnp.tanh(jnp.dot(weight_mid, hidden_one, preferred_element_type=jnp.float32) + bias_mid[:, None]).astype(jnp.bfloat16)
    closure = jnp.dot(weight_out, hidden_two, preferred_element_type=jnp.float32) + bias_out[:, None]
    return (hidden_one, hidden_two, closure)

def closure_backward(features_block, force_grad, hidden_one, hidden_two, weight_mid, weight_out):
    grad_weight_out = contract_cells(force_grad, hidden_two)
    grad_bias_out = lax.optimization_barrier(jnp.sum(force_grad.astype(jnp.float32), 1))
    back_two = jnp.dot(weight_out.T, force_grad, preferred_element_type=jnp.float32)
    two_value = hidden_two.astype(jnp.float32)
    delta_two = (back_two * (1.0 - two_value * two_value)).astype(jnp.bfloat16)
    grad_weight_mid = contract_cells(delta_two, hidden_one)
    grad_bias_mid = lax.optimization_barrier(jnp.sum(delta_two.astype(jnp.float32), 1))
    back_one = jnp.dot(weight_mid.T, delta_two, preferred_element_type=jnp.float32)
    one_value = hidden_one.astype(jnp.float32)
    delta_one = (back_one * (1.0 - one_value * one_value)).astype(jnp.bfloat16)
    grad_weight_in = contract_cells(delta_one, features_block)
    grad_bias_in = lax.optimization_barrier(jnp.sum(delta_one.astype(jnp.float32), 1))
    return (grad_weight_in, grad_bias_in, grad_weight_mid, grad_bias_mid, grad_weight_out, grad_bias_out)

def reference(velocity, target, weight_in, bias_in, weight_mid, bias_mid, weight_out, bias_out, thrust_coef, tile_cells, tile_turbine, tile_weight):
    cells_dev = CX * CY * NZ
    block_total = N_GX * N_GY
    params = (weight_in, bias_in, weight_mid, bias_mid, weight_out, bias_out)
    totals = (jnp.zeros((UNITS, FEATS), jnp.float32), jnp.zeros((UNITS,), jnp.float32), jnp.zeros((UNITS, UNITS), jnp.float32), jnp.zeros((UNITS,), jnp.float32), jnp.zeros((3, UNITS), jnp.float32), jnp.zeros((3,), jnp.float32))
    cost = jnp.zeros((), jnp.float32)
    new_fields = []
    force_fields = []
    matches = (tile_turbine[:, None] == jnp.arange(TURBINES, dtype=jnp.int32)[None, :]).astype(jnp.float32)
    cell_rows = tile_cells.reshape(block_total, TILES_DEV * DISK_ROW).astype(jnp.int32)
    weight_sums = lax.optimization_barrier(jnp.sum(tile_weight, 1))

    def forward_block(features_block):
        return closure_forward(features_block, *params)[2]

    def accumulate(carry, inputs):
        features_block, force_block = inputs
        hidden_one, hidden_two, unused = closure_forward(features_block, *params)
        grads = closure_backward(features_block, force_block, hidden_one, hidden_two, weight_mid, weight_out)
        return (jax.tree.map(lambda first_term, second_term: first_term + second_term, carry, grads), None)

    def scatter_block(rows_here, values_here):
        return jnp.zeros((cells_dev,), jnp.float32).at[rows_here].add(values_here)
    for case_index in range(CASES):
        velocity_case = velocity[case_index]
        extended = pad_all(velocity_case).astype(jnp.float32)
        gradients = [central(extended, spatial_dim) for spatial_dim in range(3)]
        fluctuation = velocity_case.astype(jnp.float32)
        full_speed = fluctuation.at[0].add(inflow)
        features = jnp.concatenate(gradients + [fluctuation], 0).astype(jnp.bfloat16)
        feature_blocks = to_blocks(features)
        closure = from_blocks(lax.map(forward_block, feature_blocks))
        stream_blocks = to_blocks(full_speed[0])
        sampled = jnp.take_along_axis(stream_blocks, cell_rows, axis=1).reshape(TILES, DISK_ROW)
        weighted = lax.optimization_barrier(jnp.sum(tile_weight * sampled, 1))
        disk_sum = lax.optimization_barrier(jnp.sum(matches * weighted[:, None], 0))
        disk_area = lax.optimization_barrier(jnp.sum(matches * weight_sums[:, None], 0))
        disk_speed = disk_sum / jnp.maximum(disk_area, 1.0)
        thrust = -0.5 * thrust_coef * disk_speed * jnp.abs(disk_speed)
        row_thrust = lax.optimization_barrier(jnp.sum(matches * thrust[None, :], 1))
        spread = (tile_weight * row_thrust[:, None]).reshape(block_total, TILES_DEV * DISK_ROW)
        turbine_force = from_blocks(jax.vmap(scatter_block)(cell_rows, spread))
        laplace = neighbour_sum(extended) - 6.0 * fluctuation
        advect = full_speed[0] * gradients[0] + full_speed[1] * gradients[1] + full_speed[2] * gradients[2]
        tendency = viscosity * laplace - advect + closure
        tendency = tendency.at[0].add(turbine_force)
        provisional = (fluctuation + step_dt * tendency).astype(jnp.bfloat16)
        rim = pad_all(provisional).astype(jnp.float32)
        updated = provisional.astype(jnp.float32) - pressure_correction(divergence_of(rim))
        new_fields.append(updated.astype(jnp.bfloat16))
        mismatch = updated - target[case_index].astype(jnp.float32)
        cost = cost + jnp.sum(mismatch * mismatch)
        seed_grad = 2.0 * mismatch
        adjoint = seed_grad - pressure_correction(divergence_of(pad_all(seed_grad)))
        force_field = (step_dt * adjoint).astype(jnp.bfloat16)
        force_fields.append(force_field)
        force_blocks = to_blocks(force_field)
        totals = lax.scan(accumulate, totals, (feature_blocks, force_blocks))[0]
    entry_total = UNITS * FEATS + UNITS + UNITS * UNITS + UNITS + 3 * UNITS + 3
    squares = sum((jnp.sum(grad_value * grad_value) for grad_value in totals))
    scale_rms = jnp.sqrt(squares / entry_total + epsilon_rms)
    loss = cost / (3 * CASES * NX * NY * NZ)
    velocity_new = jnp.stack(new_fields)
    force_grad = jnp.stack(force_fields)
    return (velocity_new, loss, totals[0] / scale_rms, totals[1] / scale_rms, totals[2] / scale_rms, totals[3] / scale_rms, totals[4] / scale_rms, totals[5] / scale_rms, force_grad)
```

```python
import functools

import jax
import jax.numpy as jnp
from jax import lax
from jax.experimental import pallas as pl
from jax.experimental.pallas import tpu as pltpu
from jax.sharding import PartitionSpec as P


ITERS = 20
INFLOW = 1.0
STEP_DT = 0.4
VISCOSITY = 0.1
EPSILON_RMS = 1e-06

F32 = jnp.float32
BF16 = jnp.bfloat16
VMEM = pltpu.VMEM
LIMIT = 58 * 1024 * 1024


def vspec():
    return pl.BlockSpec(memory_space=pltpu.VMEM)


def sspec():
    return pl.BlockSpec(memory_space=pltpu.SMEM)


def dot(a, b):
    return lax.dot_general(a, b, (((1,), (0,)), ((), ())), preferred_element_type=F32)


def dot_nt(a, b):
    return lax.dot_general(a, b, (((1,), (1,)), ((), ())), preferred_element_type=F32)


def lane_shifts(values, step=1):
    depth = values.shape[-1]
    axis = values.ndim - 1
    lane = lax.broadcasted_iota(jnp.int32, values.shape, axis)
    up = jnp.where(lane < depth - step, pltpu.roll(values, depth - step, axis), 0.0)
    down = jnp.where(lane >= step, pltpu.roll(values, step, axis), 0.0)
    return up, down


def start_kernel(odd_ref, cells_ref, turbine_ref, weight_ref, v_ref, t_ref, *outs):
    n_x_sends = (len(outs) - 1) // 2 if False else None
    del n_x_sends
    face_refs, disk_ref = outs[:-1], outs[-1]
    span_x, span_y, depth = v_ref.shape[1:]
    for ref, (dim, high_parity) in zip(face_refs, start_kernel.plan):
        take_high = odd_ref[dim] == high_parity
        for part, source in enumerate((v_ref, t_ref)):
            for c in range(3):
                if dim == 0:
                    high, low = source[c, span_x - 1], source[c, 0]
                    ref[3 * part + c] = jnp.where(take_high, high.astype(F32), low.astype(F32)).astype(BF16)
                else:
                    for x in range(span_x):
                        plane = source[c, x].astype(F32)
                        row = jnp.where(take_high, plane[span_y - 1 : span_y], plane[0:1])
                        ref[3 * part + c, x : x + 1, :] = row.astype(BF16)
    rows = span_x * span_y
    tiles, width = cells_ref.shape
    stream = v_ref[0].astype(F32).reshape(rows, depth).T.astype(BF16)
    pick = []
    for r in range(tiles):
        cell_row = cells_ref[r : r + 1, :] // depth
        spot = lax.broadcasted_iota(jnp.int32, (rows, width), 0)
        pick.append((spot == cell_row).astype(F32).astype(BF16))
    found = dot(stream, jnp.concatenate(pick, 1))
    turbines = disk_ref.shape[1]
    lane = lax.broadcasted_iota(jnp.int32, (1, turbines), 1)
    total = jnp.zeros((1, turbines), F32)
    area = jnp.zeros((1, turbines), F32)
    spot = lax.broadcasted_iota(jnp.int32, (depth, width), 0)
    for r in range(tiles):
        cell_lane = cells_ref[r : r + 1, :] % depth
        values = jnp.sum(jnp.where(spot == cell_lane, found[:, r * width : (r + 1) * width], 0.0), 0, keepdims=True)
        weight = weight_ref[r : r + 1, :]
        weighted = jnp.sum(weight * (values + INFLOW), 1, keepdims=True)
        summed = jnp.sum(weight, 1, keepdims=True)
        mine = lane == turbine_ref[r]
        total = total + jnp.where(mine, weighted, 0.0)
        area = area + jnp.where(mine, summed, 0.0)
    disk_ref[...] = jnp.zeros_like(disk_ref)
    disk_ref[0:1, :] = total
    disk_ref[1:2, :] = area


def fill_padded(pad, source, first, odd_ref, faces, plan):
    span_x, span_y = source.shape[1], source.shape[2]
    depth = source.shape[3]
    zero_plane = jnp.zeros((span_y, depth), F32)
    zero_rows = jnp.zeros((span_x, depth), F32)
    for c in range(3):
        for x in range(span_x):
            pad[c, 1 + x, 8 : 8 + span_y, :] = source[c, x].astype(F32)
        low = {0: zero_plane, 1: zero_rows}
        high = {0: zero_plane, 1: zero_rows}
        for ref, (dim, high_parity) in zip(faces, plan):
            got = ref[first + c].astype(F32)
            is_high = odd_ref[dim] == high_parity
            high[dim] = jnp.where(is_high, got, high[dim])
            low[dim] = jnp.where(is_high, low[dim], got)
        pad[c, 0, 8 : 8 + span_y, :] = low[0]
        pad[c, 1 + span_x, 8 : 8 + span_y, :] = high[0]
        for x in range(span_x):
            pad[c, 1 + x, 7:8, :] = low[1][x : x + 1]
            pad[c, 1 + x, 8 + span_y : 9 + span_y, :] = high[1][x : x + 1]


def forward_kernel(plan, n_faces, odd_ref, *refs):
    faces = refs[:n_faces]
    (v_ref, w_in, w_mid, b_mid, w_out, b_out, one_ref, two_ref, feat_ref, closure_ref, pad, stage, stage_out) = refs[n_faces:]
    span_y, depth = v_ref.shape[2], v_ref.shape[3]
    i = pl.program_id(0)

    @pl.when(i == 0)
    def _():
        fill_padded(pad, v_ref, 0, odd_ref, faces, plan)
        channel = lax.broadcasted_iota(jnp.int32, stage.shape, 0) % 16
        stage[...] = jnp.where((channel >= 12) & (channel < 15), 1.0, 0.0)

    def put(channel, value):
        stage[pl.ds(channel, span_y, stride=16), :] = value

    for c in range(3):
        centre = pad[c, i + 1, 8 : 8 + span_y, :]
        put(c, 0.5 * (pad[c, i + 2, 8 : 8 + span_y, :] - pad[c, i, 8 : 8 + span_y, :]))
        put(3 + c, 0.5 * (pad[c, i + 1, 9 : 9 + span_y, :] - pad[c, i + 1, 7 : 7 + span_y, :]))
        up, down = lane_shifts(centre)
        put(6 + c, 0.5 * (up - down))
        put(9 + c, centre)
    features = jnp.concatenate([stage[16 * y : 16 * y + 16, :].astype(BF16) for y in range(span_y)], 1)
    feat_ref[...] = features
    hidden_one = jnp.tanh(dot(w_in[...], features)).astype(BF16)
    one_ref[...] = hidden_one
    hidden_two = jnp.tanh(dot(w_mid[...], hidden_one) + b_mid[...]).astype(BF16)
    two_ref[...] = hidden_two
    out = dot(w_out[...], hidden_two) + b_out[...]
    for y in range(span_y):
        stage_out[8 * y : 8 * y + 8, :] = out[:, y * depth : (y + 1) * depth]
    for c in range(3):
        closure_ref[c, 0] = stage_out[pl.ds(c, span_y, stride=8), :]


def provisional_kernel(plan, n_faces, n_disks, odd_ref, turbine_ref, *refs):
    faces = refs[:n_faces]
    disks = refs[n_faces : n_faces + n_disks]
    (cells_ref, weight_ref, coef_ref, v_ref, t_ref, closure_ref, prov_ref, first_ref, second_ref, pad, force, qpad) = refs[
        n_faces + n_disks :
    ]
    span_x, span_y, depth = v_ref.shape[1:]
    rows = span_x * span_y
    tiles, width = cells_ref.shape
    half = span_x // 2
    sums = disks[0][...]
    for extra in disks[1:]:
        sums = sums + extra[...]
    speed = sums[0:1, :] / jnp.maximum(sums[1:2, :], 1.0)
    thrust = -0.5 * coef_ref[...] * speed * jnp.abs(speed)
    lane = lax.broadcasted_iota(jnp.int32, thrust.shape, 1)
    spot_row = lax.broadcasted_iota(jnp.int32, (rows, width), 0)
    spot_lane = lax.broadcasted_iota(jnp.int32, (depth, width), 0)
    pick, spread = [], []
    for r in range(tiles):
        row_thrust = jnp.sum(jnp.where(lane == turbine_ref[r], thrust, 0.0), 1, keepdims=True)
        strength = weight_ref[r : r + 1, :] * row_thrust
        cell = cells_ref[r : r + 1, :]
        pick.append((spot_row == cell // depth).astype(F32).astype(BF16))
        spread.append(jnp.where(spot_lane == cell % depth, strength, 0.0))
    pick = jnp.concatenate(pick, 1)
    spread = jnp.concatenate(spread, 1)
    hi = spread.astype(BF16)
    rest = spread - hi.astype(F32)
    mid = rest.astype(BF16)
    low = (rest - mid.astype(F32)).astype(BF16)
    force[...] = dot_nt(pick, hi) + (dot_nt(pick, mid) + dot_nt(pick, low))

    fill_padded(pad, t_ref, 3, odd_ref, faces, plan)
    for x in range(span_x):
        up, down = lane_shifts(pad[2, x + 1, 8 : 8 + span_y, :])
        value = (
            0.5 * (pad[0, x + 2, 8 : 8 + span_y, :] - pad[0, x, 8 : 8 + span_y, :])
            + 0.5 * (pad[1, x + 1, 9 : 9 + span_y, :] - pad[1, x + 1, 7 : 7 + span_y, :])
            + 0.5 * (up - down)
        )
        where_to = first_ref if x < half else second_ref
        where_to[half + x % half] = value

    fill_padded(pad, v_ref, 0, odd_ref, faces, plan)
    qpad[...] = jnp.zeros_like(qpad)
    for x in range(span_x):
        centre = [pad[c, x + 1, 8 : 8 + span_y, :] for c in range(3)]
        for c in range(3):
            xp, xm = pad[c, x + 2, 8 : 8 + span_y, :], pad[c, x, 8 : 8 + span_y, :]
            yp, ym = pad[c, x + 1, 9 : 9 + span_y, :], pad[c, x + 1, 7 : 7 + span_y, :]
            zp, zm = lane_shifts(centre[c])
            laplace = (xp + xm) + yp + ym + zp + zm - 6.0 * centre[c]
            advect = (
                (centre[0] + INFLOW) * (0.5 * (xp - xm)) + centre[1] * (0.5 * (yp - ym)) + centre[2] * (0.5 * (zp - zm))
            )
            tendency = VISCOSITY * laplace - advect_for(c, advect) + closure_ref[c, x]
            if c == 0:
                tendency = tendency + force[x * span_y : (x + 1) * span_y, :]
            value = (centre[c] + STEP_DT * tendency).astype(BF16)
            prov_ref[c, x] = value
            qpad[c, 1 + x, 8 : 8 + span_y, :] = value.astype(F32)
    for x in range(span_x):
        up, down = lane_shifts(qpad[2, x + 1, 8 : 8 + span_y, :])
        value = (
            0.5 * (qpad[0, x + 2, 8 : 8 + span_y, :] - qpad[0, x, 8 : 8 + span_y, :])
            + 0.5 * (qpad[1, x + 1, 9 : 9 + span_y, :] - qpad[1, x + 1, 7 : 7 + span_y, :])
            + 0.5 * (up - down)
        )
        where_to = first_ref if x < half else second_ref
        where_to[x % half] = value
        second_ref[2 * half, x : x + 1, :] = 0.5 * qpad[1, 1 + x, 8:9, :]
        second_ref[2 * half + 1, x : x + 1, :] = -0.5 * qpad[1, 1 + x, 7 + span_y : 8 + span_y, :]
    first_ref[2 * half] = 0.5 * qpad[0, 1, 8 : 8 + span_y, :]
    first_ref[2 * half + 1] = -0.5 * qpad[0, span_x, 8 : 8 + span_y, :]


def advect_for(component, advect):
    return advect


def solve_kernel(offsets, at_ref, *refs):
    n = len(offsets)
    firsts, seconds = refs[:n], refs[n : 2 * n]
    q_ref, t_ref, new_ref, grad_ref, cost_ref, div, div_t, source, pa, pb, seed = refs[2 * n :]
    span_x, span_y, depth = q_ref.shape[1:]
    total_x, total_y = source.shape[0], source.shape[1]
    half = span_x // 2
    rows = slice(8, 8 + total_y)
    ix, iy = at_ref[0], at_ref[1]

    pa[...] = jnp.zeros_like(pa)
    pb[...] = jnp.zeros_like(pb)
    spots = []
    for mx, my in offsets:
        spots.append((partner(ix, mx, total_x // span_x) * span_x, pl.multiple_of(partner(iy, my, total_y // span_y) * span_y, span_y)))
    for k, (x0, y0) in enumerate(spots):
        for ref, base in ((firsts[k], 0), (seconds[k], half)):
            for x in range(half):
                div[x0 + base + x + 1, pl.ds(pl.multiple_of(y0 + 8, 8), span_y), :] = ref[x]
                div_t[x0 + base + x, pl.ds(y0, span_y), :] = ref[half + x]
    for k, (x0, y0) in enumerate(spots):
        own = pl.ds(pl.multiple_of(y0 + 8, 8), span_y)
        div[x0, own, :] = div[x0, own, :] + firsts[k][2 * half]
        div[x0 + span_x + 1, own, :] = div[x0 + span_x + 1, own, :] + firsts[k][2 * half + 1]
        for x in range(span_x):
            below = pl.ds(y0 + 7, 1)
            above = pl.ds(y0 + 8 + span_y, 1)
            div[x0 + x + 1, below, :] = div[x0 + x + 1, below, :] + seconds[k][2 * half, x : x + 1, :]
            div[x0 + x + 1, above, :] = div[x0 + x + 1, above, :] + seconds[k][2 * half + 1, x : x + 1, :]

    unit = 1.0 / (6.0 * STEP_DT)

    def first_source(x, carry):
        value = div[x + 1, rows, :] * unit
        source[x] = value
        pa[x + 2, rows, :] = -value
        return carry

    lax.fori_loop(0, total_x, first_source, 0)

    def sweep(src, dst):
        def plane(x, carry):
            for k in range(2):
                y = 2 * x + k
                centre = src[y + 2, rows, :]
                around = src[y + 1, rows, :] + src[y + 3, rows, :]
                around = around + src[y + 2, 9 : 9 + total_y, :] + src[y + 2, 7 : 7 + total_y, :]
                up, down = lane_shifts(centre)
                dst[y + 2, rows, :] = (around + up + down) * (1.0 / 6.0) - source[y]
            return carry

        lax.fori_loop(0, total_x // 2, plane, 0)

    def sweeps():
        def two(k, carry):
            sweep(pa, pb)
            sweep(pb, pa)
            return carry

        lax.fori_loop(0, (ITERS - 1) // 2, two, 0)
        if (ITERS - 1) % 2:
            sweep(pa, pb)
            return pb
        return pa

    def correction(p, x):
        at = ix * span_x + x + 2
        y0 = pl.multiple_of(iy * span_y, 8)
        own = pl.ds(pl.multiple_of(y0 + 8, 8), span_y)
        wide = p[at, pl.ds(y0, span_y + 16), :]
        up, down = lane_shifts(wide[8 : 8 + span_y])
        return (
            STEP_DT * (0.5 * (p[at + 1, own, :] - p[at - 1, own, :])),
            STEP_DT * (0.5 * (wide[9 : 9 + span_y] - wide[7 : 7 + span_y])),
            STEP_DT * (0.5 * (up - down)),
        )

    p = sweeps()
    cost = jnp.zeros((span_y, depth), F32)
    for x in range(span_x):
        moves = correction(p, x)
        for c in range(3):
            updated = q_ref[c, x].astype(F32) - moves[c]
            new_ref[c, x] = updated.astype(BF16)
            mismatch = updated - t_ref[c, x].astype(F32)
            cost = cost + mismatch * mismatch
            seed[c, x] = 2.0 * mismatch
    cost_ref[...] = cost[0:8] + sum((cost[k : k + 8] for k in range(8, span_y, 8)), jnp.zeros((8, depth), F32))

    def second_source(x, carry):
        centre = p[x + 2, rows, :]
        to_high = jnp.where(x + 1 < total_x, 0.25, 0.0)
        to_low = jnp.where(x > 0, 0.25, 0.0)
        wide = to_high * (p[x + 4, rows, :] - centre) - to_low * (centre - p[x, rows, :])
        row = lax.broadcasted_iota(jnp.int32, centre.shape, 0)
        lane = lax.broadcasted_iota(jnp.int32, centre.shape, 1)
        wide = wide + 0.25 * (
            jnp.where(row < total_y - 1, p[x + 2, 10 : 10 + total_y, :] - centre, 0.0)
            - jnp.where(row > 0, centre - p[x + 2, 6 : 6 + total_y, :], 0.0)
        )
        up, down = lane_shifts(centre, 2)
        wide = wide + 0.25 * (
            jnp.where(lane < depth - 1, up - centre, 0.0) - jnp.where(lane > 0, centre - down, 0.0)
        )
        value = (2.0 * unit) * (div[x + 1, rows, :] - STEP_DT * wide - div_t[x])
        source[x] = value
        return carry

    lax.fori_loop(0, total_x, second_source, 0)

    def restart(x, carry):
        pa[x + 2, rows, :] = -source[x]
        return carry

    lax.fori_loop(0, total_x, restart, 0)
    p = sweeps()
    for x in range(span_x):
        moves = correction(p, x)
        for c in range(3):
            grad_ref[c, x] = (STEP_DT * (seed[c, x] - moves[c])).astype(BF16)


def backward_kernel(grad_ref, feat_ref, one_ref, two_ref, w_out_t, w_mid_t, cost_ref, sum_ref, stage, acc_mid, acc_in, acc_out, acc_b):
    span_y, depth = grad_ref.shape[2], grad_ref.shape[3]
    units = one_ref.shape[0]
    i = pl.program_id(0)

    @pl.when(i == 0)
    def _():
        stage[...] = jnp.zeros_like(stage)
        acc_mid[...] = jnp.zeros_like(acc_mid)
        acc_in[...] = jnp.zeros_like(acc_in)
        acc_out[...] = jnp.zeros_like(acc_out)
        acc_b[...] = jnp.zeros_like(acc_b)

    for c in range(3):
        stage[pl.ds(c, span_y, stride=16), :] = grad_ref[c, 0].astype(F32)
    grad = jnp.concatenate([stage[16 * y : 16 * y + 16, :].astype(BF16) for y in range(span_y)], 1)
    bias = stage[0:8, :]
    for y in range(1, span_y):
        bias = bias + stage[16 * y : 16 * y + 8, :]
    acc_b[...] += bias
    hidden_one, hidden_two = one_ref[...], two_ref[...]
    acc_out[...] += dot_nt(grad, hidden_two)
    two_value = hidden_two.astype(F32)
    delta_two = (dot(w_out_t[...], grad) * (1.0 - two_value * two_value)).astype(BF16)
    ones = jnp.ones((16, hidden_one.shape[1]), BF16)
    acc_mid[...] += dot_nt(jnp.concatenate([hidden_one, ones], 0), delta_two)
    one_value = hidden_one.astype(F32)
    delta_one = (dot(w_mid_t[...], delta_two) * (1.0 - one_value * one_value)).astype(BF16)
    acc_in[...] += dot_nt(feat_ref[...], delta_one)

    @pl.when(i == pl.num_programs(0) - 1)
    def _():
        sum_ref[...] = jnp.zeros_like(sum_ref)
        sum_ref[0:units, :] = acc_mid[0:units, :]
        sum_ref[units : units + 13, :] = acc_in[0:13, :]
        sum_ref[units + 13 : units + 14, :] = acc_mid[units : units + 1, :]
        sum_ref[units + 14 : units + 17, :] = acc_out[0:3, :]
        lane = lax.broadcasted_iota(jnp.int32, (1, units), 1)
        row = jnp.where(lane == 3, jnp.sum(cost_ref[...]), 0.0)
        for c in range(3):
            row = row + jnp.where(lane == c, jnp.sum(acc_b[c : c + 1, :]), 0.0)
        sum_ref[units + 17 : units + 18, :] = row


def finish_kernel(offsets, entry_total, cell_total, at_ref, *refs):
    n = len(offsets)
    pieces = refs[:n]
    loss_ref, in_ref, b_in_ref, mid_ref, b_mid_ref, out_ref, b_out_ref, whole = refs[n:]
    units = mid_ref.shape[0]
    feats = in_ref.shape[1]
    size = pieces[0].shape[0]
    for ref, spot in zip(pieces, offsets):
        whole[pl.ds(pl.multiple_of(at_ref[spot] * size, 8), size), :] = ref[...]
    mid = whole[0:units, :]
    small = whole[units : units + 32, :]
    row = lax.broadcasted_iota(jnp.int32, small.shape, 0)
    lane = lax.broadcasted_iota(jnp.int32, small.shape, 1)
    counted = (row < feats + 5) | ((row == feats + 5) & (lane < 3))
    squares = jnp.sum(mid * mid) + jnp.sum(jnp.where(counted, small * small, 0.0))
    scale = jnp.full((1, 1), 1.0, F32) / jnp.sqrt(jnp.full((1, 1), 1.0, F32) * squares / entry_total + EPSILON_RMS)
    small = small * scale
    mid_ref[...] = (mid * scale).T
    in_ref[...] = small.T[:, 0:feats]
    b_in_ref[...] = small[feats : feats + 1]
    b_mid_ref[...] = small[feats + 1 : feats + 2]
    out_ref[...] = small[feats + 2 : feats + 5]
    b_out_ref[...] = small[feats + 5 : feats + 6, 0:3]
    loss_ref[...] = whole[units + feats + 5 : units + feats + 6, 3:4] / cell_total


def is_power(count):
    return count & (count - 1) == 0


def partner(index, step, count):
    return index ^ step if is_power(count) else (index + step) % count


def pair_list(count, offset):
    pairs = []
    for low in range(offset, count - 1, 2):
        pairs += [(low, low + 1), (low + 1, low)]
    return pairs


def face_plan(n_x, n_y):
    plan = []
    for dim, count in ((0, n_x), (1, n_y)):
        if count > 1:
            plan.append((dim, 0))
        if count > 2:
            plan.append((dim, 1))
    return tuple(plan)


def swap(values, axis, step):
    count = lax.axis_size(axis)
    return lax.ppermute(values, axis, [(i, partner(i, step, count)) for i in range(count)])


def swap_both(values, step_x, step_y):
    n_x, n_y = lax.axis_size("gx"), lax.axis_size("gy")
    pairs = [
        (i * n_y + j, partner(i, step_x, n_x) * n_y + partner(j, step_y, n_y)) for i in range(n_x) for j in range(n_y)
    ]
    return lax.ppermute(values, ("gx", "gy"), pairs)


def gather_doubling(values, order):
    held = {(0, 0): values}
    for axis, bit in order:
        for (sx, sy), block in list(held.items()):
            key = (sx ^ bit, sy) if axis == "gx" else (sx, sy ^ bit)
            held[key] = swap(block, axis, bit)
    return held


def bits_of(axis, count):
    return [(axis, 1 << k) for k in reversed(range(count.bit_length() - 1))]


def on_device(
    velocity,
    target,
    weight_in,
    bias_in,
    weight_mid,
    bias_mid,
    weight_out,
    bias_out,
    thrust_coef,
    tile_cells,
    tile_turbine,
    tile_weight,
):
    v, t = velocity[0], target[0]
    _, span_x, span_y, depth = v.shape
    units, feats = weight_in.shape
    cells = span_x * span_y * depth
    turbines = thrust_coef.shape[0]
    n_case, n_x, n_y = lax.axis_size("case"), lax.axis_size("gx"), lax.axis_size("gy")
    ix, iy = lax.axis_index("gx"), lax.axis_index("gy")
    at = jnp.stack([ix, iy]).astype(jnp.int32)
    odd = at & 1
    plan = face_plan(n_x, n_y)
    shape_of = jax.ShapeDtypeStruct

    start_kernel.plan = plan
    started = pl.pallas_call(
        start_kernel,
        name="start",
        out_shape=tuple(shape_of((6, span_y if d == 0 else span_x, depth), BF16) for d, _ in plan)
        + (shape_of((8, turbines), F32),),
        in_specs=[sspec(), vspec(), sspec(), vspec(), vspec(), vspec()],
        out_specs=tuple(vspec() for _ in range(len(plan) + 1)),
        compiler_params=pltpu.CompilerParams(vmem_limit_bytes=LIMIT),
    )(odd, tile_cells, tile_turbine, tile_weight, v, t)
    disk = started[-1]
    faces = []
    for face, (dim, parity) in zip(started[:-1], plan):
        axis, count = (("gx", n_x), ("gy", n_y))[dim]
        faces.append(lax.ppermute(face, axis, pair_list(count, parity)))
    if n_y > 1 and is_power(n_y) and is_power(n_x):
        disk = disk + swap(disk, "gy", 1)
        disks = [disk] + [
            swap_both(disk, a, b) for a in range(n_x) for b in range(0, n_y, 2) if (a, b) != (0, 0)
        ]
    else:
        disks = [swap_both(disk, a, b) for a in range(n_x) for b in range(n_y)]

    b_hi = lax.reduce_precision(bias_in, 8, 7)
    b_mid_part = lax.reduce_precision(bias_in - b_hi, 8, 7)
    b_low = bias_in - b_hi - b_mid_part
    w_in = jnp.concatenate(
        [weight_in] + [part[:, None].astype(BF16) for part in (b_hi, b_mid_part, b_low, jnp.zeros_like(b_hi))], 1
    )
    w_out = jnp.pad(weight_out, ((0, 5), (0, 0)))
    b_out = jnp.pad(bias_out, (0, 5))[:, None]
    w_out_t = jnp.pad(weight_out, ((0, 13), (0, 0))).T
    w_mid_t = weight_mid.T

    whole = lambda shape: pl.BlockSpec(shape, lambda i: (0,) * len(shape))
    chunk = span_y * depth
    face_shape = [f.shape for f in faces]
    hidden_one, hidden_two, features, closure = pl.pallas_call(
        functools.partial(forward_kernel, plan, len(faces)),
        name="closure_forward",
        grid=(span_x,),
        out_shape=(
            shape_of((units, cells), BF16),
            shape_of((units, cells), BF16),
            shape_of((16, cells), BF16),
            shape_of((3, span_x, span_y, depth), F32),
        ),
        in_specs=[sspec()]
        + [whole(s) for s in face_shape]
        + [
            whole(v.shape),
            whole(w_in.shape),
            whole(weight_mid.shape),
            whole((units, 1)),
            whole(w_out.shape),
            whole(b_out.shape),
        ],
        out_specs=(
            pl.BlockSpec((units, chunk), lambda i: (0, i)),
            pl.BlockSpec((units, chunk), lambda i: (0, i)),
            pl.BlockSpec((16, chunk), lambda i: (0, i)),
            pl.BlockSpec((3, 1, span_y, depth), lambda i: (0, i, 0, 0)),
        ),
        scratch_shapes=[
            VMEM((3, span_x + 2, span_y + 16, depth), F32),
            VMEM((16 * span_y, depth), F32),
            VMEM((8 * span_y, depth), F32),
        ],
        compiler_params=pltpu.CompilerParams(vmem_limit_bytes=LIMIT),
    )(odd, *faces, v, w_in, weight_mid, bias_mid[:, None], w_out, b_out)

    message = shape_of((span_x + 2, span_y, depth), F32)
    prov, first, second = pl.pallas_call(
        functools.partial(provisional_kernel, plan, len(faces), len(disks)),
        name="provisional",
        out_shape=(shape_of(v.shape, BF16), message, message),
        in_specs=[sspec(), sspec()] + [vspec() for _ in range(len(faces) + len(disks) + 6)],
        out_specs=(vspec(), vspec(), vspec()),
        scratch_shapes=[
            VMEM((3, span_x + 2, span_y + 16, depth), F32),
            VMEM((span_x * span_y, depth), F32),
            VMEM((3, span_x + 2, span_y + 16, depth), F32),
        ],
        compiler_params=pltpu.CompilerParams(vmem_limit_bytes=LIMIT),
    )(odd, tile_turbine, *faces, *disks, tile_cells, tile_weight, thrust_coef.reshape(1, turbines), v, t, closure)

    if is_power(n_x) and is_power(n_y):
        x_bits, y_bits = bits_of("gx", n_x), bits_of("gy", n_y)
        firsts = gather_doubling(first, x_bits + y_bits)
        seconds = gather_doubling(second, y_bits[:-1] + x_bits + y_bits[-1:])
    else:
        steps = [(a, b) for a in range(n_x) for b in range(n_y)]
        firsts = {s: swap_both(first, *s) for s in steps}
        seconds = {s: swap_both(second, *s) for s in steps}
    offsets = sorted(firsts)
    total_x, total_y = n_x * span_x, n_y * span_y
    new, force_field, cost = pl.pallas_call(
        functools.partial(solve_kernel, tuple(offsets)),
        name="solve",
        out_shape=(shape_of(v.shape, BF16), shape_of(v.shape, BF16), shape_of((8, depth), F32)),
        in_specs=[sspec()] + [vspec() for _ in range(2 * len(offsets) + 2)],
        out_specs=(vspec(), vspec(), vspec()),
        scratch_shapes=[
            VMEM((total_x + 2, total_y + 16, depth), F32),
            VMEM((total_x, total_y, depth), F32),
            VMEM((total_x, total_y, depth), F32),
            VMEM((total_x + 4, total_y + 16, depth), F32),
            VMEM((total_x + 4, total_y + 16, depth), F32),
            VMEM((3, span_x, span_y, depth), F32),
        ],
        compiler_params=pltpu.CompilerParams(vmem_limit_bytes=LIMIT),
    )(at, *[firsts[o] for o in offsets], *[seconds[o] for o in offsets], prov, t)

    n_pieces = n_x * n_y
    total_rows = -(-(units + 32) // (8 * n_pieces)) * 8 * n_pieces
    sums = pl.pallas_call(
        backward_kernel,
        name="closure_backward",
        grid=(span_x,),
        out_shape=shape_of((total_rows, units), F32),
        in_specs=[
            pl.BlockSpec((3, 1, span_y, depth), lambda i: (0, i, 0, 0)),
            pl.BlockSpec((16, chunk), lambda i: (0, i)),
            pl.BlockSpec((units, chunk), lambda i: (0, i)),
            pl.BlockSpec((units, chunk), lambda i: (0, i)),
            whole(w_out_t.shape),
            whole(w_mid_t.shape),
            whole((8, depth)),
        ],
        out_specs=whole((total_rows, units)),
        scratch_shapes=[
            VMEM((16 * span_y, depth), F32),
            VMEM((units + 16, units), F32),
            VMEM((16, units), F32),
            VMEM((16, units), F32),
            VMEM((8, depth), F32),
        ],
        compiler_params=pltpu.CompilerParams(vmem_limit_bytes=LIMIT),
    )(force_field, features, hidden_one, hidden_two, w_out_t, w_mid_t, cost)

    if n_y > 1 and is_power(n_x) and is_power(n_y) and is_power(n_case):
        group = n_pieces // 2
        size = total_rows // n_pieces
        sums = sums + swap(sums, "gy", 1)
        mine = lax.dynamic_slice_in_dim(sums, (iy & 1) * (group * size), group * size, 0)
        steps = [(a, b) for a in range(n_x) for b in range(0, n_y, 2)]
        spot = lambda a, b: (ix ^ a) * (n_y // 2) + ((iy ^ b) >> 1)
        cut = lambda s: lax.dynamic_slice_in_dim(mine, spot(*s) * size, size, 0)
        piece = cut((0, 0))
        for s in steps[1:]:
            piece = piece + swap_both(cut(s), *s)
        others = [swap(piece, "case", m) for m in range(1, n_case)]
        for other in others:
            piece = piece + other
        here = [piece] + [swap_both(piece, *s) for s in steps[1:]]
        there = [swap(p, "gy", 1) for p in here]
        pieces = here + there
        spots = [(iy & 1) * group + spot(*s) for s in steps] + [(1 - (iy & 1)) * group + spot(*s) for s in steps]
    else:
        pieces = [lax.psum(sums, ("case", "gx", "gy"))]
        spots = [jnp.zeros((), jnp.int32)]
    places = jnp.stack(spots).astype(jnp.int32)

    entry_total = units * feats + units + units * units + units + 3 * units + 3
    cell_total = 3 * cells * n_case * n_x * n_y
    loss, s_in, sb_in, s_mid, sb_mid, s_out, sb_out = pl.pallas_call(
        functools.partial(finish_kernel, tuple(range(len(pieces))), entry_total, cell_total),
        name="finish",
        out_shape=(
            shape_of((1, 1), F32),
            shape_of((units, feats), F32),
            shape_of((1, units), F32),
            shape_of((units, units), F32),
            shape_of((1, units), F32),
            shape_of((3, units), F32),
            shape_of((1, 3), F32),
        ),
        in_specs=[sspec()] + [vspec() for _ in pieces],
        out_specs=tuple(vspec() for _ in range(7)),
        scratch_shapes=[VMEM((total_rows, units), F32)],
        compiler_params=pltpu.CompilerParams(vmem_limit_bytes=LIMIT),
    )(places, *pieces)
    return (
        new[None],
        loss.reshape(()),
        s_in,
        sb_in.reshape(units),
        s_mid,
        sb_mid.reshape(units),
        s_out,
        sb_out.reshape(3),
        force_field[None],
    )


def solution(mesh):
    placed = (
        P("case", None, "gx", "gy", None),
        P("case", None, "gx", "gy", None),
        P(),
        P(),
        P(),
        P(),
        P(),
        P(),
        P(),
        P(("gx", "gy"), None),
        P(("gx", "gy")),
        P(("gx", "gy"), None),
    )
    field = P("case", None, "gx", "gy", None)
    return jax.shard_map(
        on_device,
        mesh=mesh,
        in_specs=placed,
        out_specs=(field, P(), P(), P(), P(), P(), P(), P(), field),
        check_vma=False,
    )
```

```python
import functools

import jax
import jax.numpy as jnp
from jax import lax
from jax.experimental import pallas as pl
from jax.experimental.pallas import tpu as pltpu
from jax.sharding import PartitionSpec as P


ITERS = 20
INFLOW = 1.0
STEP_DT = 0.4
VISCOSITY = 0.1
EPSILON_RMS = 1e-06

F32 = jnp.float32
BF16 = jnp.bfloat16
VMEM = pltpu.VMEM
LIMIT = 58 * 1024 * 1024


def parity_of(dim):
    return lax.axis_index(("gx", "gy")[dim]) & 1


def vspec():
    return pl.BlockSpec(memory_space=pltpu.VMEM)


def sspec():
    return pl.BlockSpec(memory_space=pltpu.SMEM)


def dot(a, b):
    return lax.dot_general(a, b, (((1,), (0,)), ((), ())), preferred_element_type=F32)


def dot_nt(a, b):
    return lax.dot_general(a, b, (((1,), (1,)), ((), ())), preferred_element_type=F32)


def lane_shifts(values, step=1):
    depth = values.shape[-1]
    axis = values.ndim - 1
    lane = lax.broadcasted_iota(jnp.int32, values.shape, axis)
    up = jnp.where(lane < depth - step, pltpu.roll(values, depth - step, axis), 0.0)
    down = jnp.where(lane >= step, pltpu.roll(values, step, axis), 0.0)
    return up, down


def start_kernel(cells_ref, turbine_ref, weight_ref, v_ref, t_ref, *outs):
    n_x_sends = (len(outs) - 1) // 2 if False else None
    del n_x_sends
    face_refs, disk_ref = outs[:-1], outs[-1]
    span_x, span_y, depth = v_ref.shape[1:]
    for ref, (dim, high_parity) in zip(face_refs, start_kernel.plan):
        take_high = parity_of(dim) == high_parity
        for part, source in enumerate((v_ref, t_ref)):
            for c in range(3):
                if dim == 0:
                    high, low = source[c, span_x - 1], source[c, 0]
                    ref[3 * part + c] = jnp.where(take_high, high.astype(F32), low.astype(F32)).astype(BF16)
                else:
                    for x in range(span_x):
                        plane = source[c, x].astype(F32)
                        row = jnp.where(take_high, plane[span_y - 1 : span_y], plane[0:1])
                        ref[3 * part + c, x : x + 1, :] = row.astype(BF16)
    rows = span_x * span_y
    tiles, width = cells_ref.shape
    stream = v_ref[0].astype(F32).reshape(rows, depth).T.astype(BF16)
    pick = []
    for r in range(tiles):
        cell_row = cells_ref[r : r + 1, :] // depth
        spot = lax.broadcasted_iota(jnp.int32, (rows, width), 0)
        pick.append((spot == cell_row).astype(F32).astype(BF16))
    found = dot(stream, jnp.concatenate(pick, 1))
    turbines = disk_ref.shape[1]
    lane = lax.broadcasted_iota(jnp.int32, (1, turbines), 1)
    total = jnp.zeros((1, turbines), F32)
    area = jnp.zeros((1, turbines), F32)
    spot = lax.broadcasted_iota(jnp.int32, (depth, width), 0)
    for r in range(tiles):
        cell_lane = cells_ref[r : r + 1, :] % depth
        values = jnp.sum(jnp.where(spot == cell_lane, found[:, r * width : (r + 1) * width], 0.0), 0, keepdims=True)
        weight = weight_ref[r : r + 1, :]
        weighted = jnp.sum(weight * (values + INFLOW), 1, keepdims=True)
        summed = jnp.sum(weight, 1, keepdims=True)
        mine = lane == turbine_ref[r]
        total = total + jnp.where(mine, weighted, 0.0)
        area = area + jnp.where(mine, summed, 0.0)
    disk_ref[...] = jnp.zeros_like(disk_ref)
    disk_ref[0:1, :] = total
    disk_ref[1:2, :] = area


def fill_padded(pad, source, first, faces, plan):
    span_x, span_y = source.shape[1], source.shape[2]
    depth = source.shape[3]
    zero_plane = jnp.zeros((span_y, depth), F32)
    zero_rows = jnp.zeros((span_x, depth), F32)
    for c in range(3):
        for x in range(span_x):
            pad[c, 1 + x, 8 : 8 + span_y, :] = source[c, x].astype(F32)
        low = {0: zero_plane, 1: zero_rows}
        high = {0: zero_plane, 1: zero_rows}
        for ref, (dim, high_parity) in zip(faces, plan):
            got = ref[first + c].astype(F32)
            is_high = parity_of(dim) == high_parity
            high[dim] = jnp.where(is_high, got, high[dim])
            low[dim] = jnp.where(is_high, low[dim], got)
        pad[c, 0, 8 : 8 + span_y, :] = low[0]
        pad[c, 1 + span_x, 8 : 8 + span_y, :] = high[0]
        for x in range(span_x):
            pad[c, 1 + x, 7:8, :] = low[1][x : x + 1]
            pad[c, 1 + x, 8 + span_y : 9 + span_y, :] = high[1][x : x + 1]


def forward_kernel(plan, n_faces, *refs):
    faces = refs[:n_faces]
    (
        v_ref, w_in_t, b_in, w_mid, b_mid, w_out, b_out,
        one_ref, two_ref, feat_ref, closure_ref,
        pad, stage, stage_out, w_in, b_column,
    ) = refs[n_faces:]
    span_y, depth = v_ref.shape[2], v_ref.shape[3]
    planes = closure_ref.shape[1]
    lines = planes * span_y
    i = pl.program_id(0)

    @pl.when(i == 0)
    def _():
        fill_padded(pad, v_ref, 0, faces, plan)
        channel = lax.broadcasted_iota(jnp.int32, stage.shape, 0) % 16
        stage[...] = jnp.where((channel >= 12) & (channel < 15), 1.0, 0.0)
        bias = b_in[...]
        high = bias.astype(BF16).astype(F32)
        rest = bias - high
        middle = rest.astype(BF16).astype(F32)
        rows = jnp.concatenate([w_in_t[...].astype(F32), high, middle, rest - middle, jnp.zeros_like(bias)], 0)
        w_in[...] = rows.T.astype(BF16)
        b_column[...] = jnp.broadcast_to(b_mid[...], (8, bias.shape[1])).T

    for k in range(planes):
        x = i * planes + k
        own = slice(8, 8 + span_y)

        def put(channel, value):
            stage[pl.ds(16 * span_y * k + channel, span_y, stride=16), :] = value

        for c in range(3):
            centre = pad[c, x + 1, own, :]
            put(c, 0.5 * (pad[c, x + 2, own, :] - pad[c, x, own, :]))
            put(3 + c, 0.5 * (pad[c, x + 1, 9 : 9 + span_y, :] - pad[c, x + 1, 7 : 7 + span_y, :]))
            up, down = lane_shifts(centre)
            put(6 + c, 0.5 * (up - down))
            put(9 + c, centre)
    features = jnp.concatenate([stage[16 * y : 16 * y + 16, :].astype(BF16) for y in range(lines)], 1)
    feat_ref[...] = features
    hidden_one = jnp.tanh(dot(w_in[...], features)).astype(BF16)
    one_ref[...] = hidden_one
    hidden_two = jnp.tanh(dot(w_mid[...], hidden_one) + b_column[:, 0:1]).astype(BF16)
    two_ref[...] = hidden_two
    out = dot(w_out[...], hidden_two)
    for y in range(lines):
        stage_out[8 * y : 8 * y + 3, :] = out[:, y * depth : (y + 1) * depth]
    for k in range(planes):
        for c in range(3):
            closure_ref[c, k] = stage_out[pl.ds(8 * span_y * k + c, span_y, stride=8), :] + b_out[c]


def provisional_kernel(plan, n_faces, n_disks, turbine_ref, *refs):
    faces = refs[:n_faces]
    disks = refs[n_faces : n_faces + n_disks]
    (cells_ref, weight_ref, coef_ref, v_ref, t_ref, closure_ref, prov_ref, first_ref, second_ref, pad, force, qpad) = refs[
        n_faces + n_disks :
    ]
    span_x, span_y, depth = v_ref.shape[1:]
    rows = span_x * span_y
    tiles, width = cells_ref.shape
    half = span_x // 2
    sums = disks[0][...]
    for extra in disks[1:]:
        sums = sums + extra[...]
    speed = sums[0:1, :] / jnp.maximum(sums[1:2, :], 1.0)
    thrust = -0.5 * coef_ref[...] * speed * jnp.abs(speed)
    lane = lax.broadcasted_iota(jnp.int32, thrust.shape, 1)
    spot_row = lax.broadcasted_iota(jnp.int32, (rows, width), 0)
    spot_lane = lax.broadcasted_iota(jnp.int32, (depth, width), 0)
    pick, spread = [], []
    for r in range(tiles):
        row_thrust = jnp.sum(jnp.where(lane == turbine_ref[r], thrust, 0.0), 1, keepdims=True)
        strength = weight_ref[r : r + 1, :] * row_thrust
        cell = cells_ref[r : r + 1, :]
        pick.append((spot_row == cell // depth).astype(F32).astype(BF16))
        spread.append(jnp.where(spot_lane == cell % depth, strength, 0.0))
    pick = jnp.concatenate(pick, 1)
    spread = jnp.concatenate(spread, 1)
    hi = spread.astype(BF16)
    rest = spread - hi.astype(F32)
    mid = rest.astype(BF16)
    low = (rest - mid.astype(F32)).astype(BF16)
    force[...] = dot_nt(pick, hi) + (dot_nt(pick, mid) + dot_nt(pick, low))

    fill_padded(pad, t_ref, 3, faces, plan)
    for x in range(span_x):
        up, down = lane_shifts(pad[2, x + 1, 8 : 8 + span_y, :])
        value = (
            0.5 * (pad[0, x + 2, 8 : 8 + span_y, :] - pad[0, x, 8 : 8 + span_y, :])
            + 0.5 * (pad[1, x + 1, 9 : 9 + span_y, :] - pad[1, x + 1, 7 : 7 + span_y, :])
            + 0.5 * (up - down)
        )
        where_to = first_ref if x < half else second_ref
        where_to[half + x % half] = value

    fill_padded(pad, v_ref, 0, faces, plan)
    qpad[...] = jnp.zeros_like(qpad)
    for x in range(span_x):
        centre = [pad[c, x + 1, 8 : 8 + span_y, :] for c in range(3)]
        for c in range(3):
            xp, xm = pad[c, x + 2, 8 : 8 + span_y, :], pad[c, x, 8 : 8 + span_y, :]
            yp, ym = pad[c, x + 1, 9 : 9 + span_y, :], pad[c, x + 1, 7 : 7 + span_y, :]
            zp, zm = lane_shifts(centre[c])
            laplace = (xp + xm) + yp + ym + zp + zm - 6.0 * centre[c]
            advect = (
                (centre[0] + INFLOW) * (0.5 * (xp - xm)) + centre[1] * (0.5 * (yp - ym)) + centre[2] * (0.5 * (zp - zm))
            )
            tendency = VISCOSITY * laplace - advect + closure_ref[c, x]
            if c == 0:
                tendency = tendency + force[x * span_y : (x + 1) * span_y, :]
            value = (centre[c] + STEP_DT * tendency).astype(BF16)
            prov_ref[c, x] = value
            qpad[c, 1 + x, 8 : 8 + span_y, :] = value.astype(F32)
    for x in range(span_x):
        up, down = lane_shifts(qpad[2, x + 1, 8 : 8 + span_y, :])
        value = (
            0.5 * (qpad[0, x + 2, 8 : 8 + span_y, :] - qpad[0, x, 8 : 8 + span_y, :])
            + 0.5 * (qpad[1, x + 1, 9 : 9 + span_y, :] - qpad[1, x + 1, 7 : 7 + span_y, :])
            + 0.5 * (up - down)
        )
        where_to = first_ref if x < half else second_ref
        where_to[x % half] = value
        second_ref[2 * half, x : x + 1, :] = 0.5 * qpad[1, 1 + x, 8:9, :]
        second_ref[2 * half + 1, x : x + 1, :] = -0.5 * qpad[1, 1 + x, 7 + span_y : 8 + span_y, :]
    first_ref[2 * half] = 0.5 * qpad[0, 1, 8 : 8 + span_y, :]
    first_ref[2 * half + 1] = -0.5 * qpad[0, span_x, 8 : 8 + span_y, :]


def solve_kernel(offsets, n_x, n_y, *refs):
    n = len(offsets)
    firsts, seconds = refs[:n], refs[n : 2 * n]
    q_ref, t_ref, new_ref, grad_ref, cost_ref, div, div_t, source, pa, pb, seed = refs[2 * n :]
    span_x, span_y, depth = q_ref.shape[1:]
    total_x, total_y = source.shape[0], source.shape[1]
    half = span_x // 2
    rows = slice(8, 8 + total_y)
    ix, iy = lax.axis_index("gx"), lax.axis_index("gy")

    pa[...] = jnp.zeros_like(pa)
    pb[...] = jnp.zeros_like(pb)
    spots = []
    for mx, my in offsets:
        spots.append((partner(ix, mx, total_x // span_x) * span_x, pl.multiple_of(partner(iy, my, total_y // span_y) * span_y, span_y)))
    for k, (x0, y0) in enumerate(spots):
        for ref, base in ((firsts[k], 0), (seconds[k], half)):
            for x in range(half):
                div[x0 + base + x + 1, pl.ds(pl.multiple_of(y0 + 8, 8), span_y), :] = ref[x]
                div_t[x0 + base + x, pl.ds(y0, span_y), :] = ref[half + x]
    for k, (x0, y0) in enumerate(spots):
        own = pl.ds(pl.multiple_of(y0 + 8, 8), span_y)
        div[x0, own, :] = div[x0, own, :] + firsts[k][2 * half]
        div[x0 + span_x + 1, own, :] = div[x0 + span_x + 1, own, :] + firsts[k][2 * half + 1]
        for x in range(span_x):
            below = pl.ds(y0 + 7, 1)
            above = pl.ds(y0 + 8 + span_y, 1)
            div[x0 + x + 1, below, :] = div[x0 + x + 1, below, :] + seconds[k][2 * half, x : x + 1, :]
            div[x0 + x + 1, above, :] = div[x0 + x + 1, above, :] + seconds[k][2 * half + 1, x : x + 1, :]

    unit = 1.0 / (6.0 * STEP_DT)

    def first_source(x, carry):
        value = div[x + 1, rows, :] * unit
        source[x] = value
        pa[x + 2, rows, :] = -value
        return carry

    lax.fori_loop(0, total_x, first_source, 0, unroll=4)

    def sweep(src, dst, x_start, x_count, y_start, y_count):
        own = pl.ds(y_start + 8, y_count)
        lane = lax.broadcasted_iota(jnp.int32, (y_count, depth), 1)
        top, bottom = lane < depth - 1, lane > 0
        group = x_count if x_count <= 32 else 32

        def planes(i, carry):
            base = x_start + i * group
            loaded = {}

            def plane(k):
                if k not in loaded:
                    loaded[k] = src[base + k, own, :]
                return loaded[k]

            for k in range(group):
                centre = plane(k + 2)
                around = plane(k + 1) + plane(k + 3)
                around = around + src[base + k + 2, pl.ds(y_start + 9, y_count), :]
                around = around + src[base + k + 2, pl.ds(y_start + 7, y_count), :]
                around = around + jnp.where(top, pltpu.roll(centre, depth - 1, 1), 0.0)
                around = around + jnp.where(bottom, pltpu.roll(centre, 1, 1), 0.0)
                dst[base + k + 2, own, :] = around * (1.0 / 6.0) - source[base + k, pl.ds(y_start, y_count), :]
                loaded.pop(k + 1)
            return carry

        if x_count == group:
            planes(0, 0)
        else:
            lax.fori_loop(0, x_count // group, planes, 0)

    def run(stages, start=0):
        buffers, now = (pa, pb), start
        for window, count in stages:

            def two(k, carry, now=now, window=window):
                sweep(buffers[now], buffers[1 - now], *window)
                sweep(buffers[1 - now], buffers[now], *window)
                return carry

            if count // 2:
                lax.fori_loop(0, count // 2, two, 0)
            if count % 2:
                sweep(buffers[now], buffers[1 - now], *window)
                now = 1 - now
        return buffers[now]

    whole = (0, total_x, 0, total_y)

    def windows():
        stages = []
        left = ITERS - 1
        for k in range(left):
            margin = -(-(left - k) // 8) * 8
            x_count = min(total_x, span_x + margin * min(n_x - 1, 2))
            y_count = min(total_y, span_y + margin * min(n_y - 1, 2))
            key = (margin, x_count, y_count)
            if stages and (stages[-1][0][1:] == key[1:]):
                stages[-1][1] += 1
            else:
                stages.append([key, 1])
        result = []
        for (margin, x_count, y_count), count in stages:
            x_start = 0 if x_count == total_x else jnp.clip(ix * span_x - margin, 0, total_x - x_count)
            y_start = 0
            if y_count != total_y:
                y_start = pl.multiple_of(jnp.clip(iy * span_y - margin, 0, total_y - y_count), 8)
            result.append(((x_start, x_count, y_start, y_count), count))
        return result

    def correction(p, x):
        at = ix * span_x + x + 2
        y0 = pl.multiple_of(iy * span_y, 8)
        own = pl.ds(pl.multiple_of(y0 + 8, 8), span_y)
        wide = p[at, pl.ds(y0, span_y + 16), :]
        up, down = lane_shifts(wide[8 : 8 + span_y])
        return (
            STEP_DT * (0.5 * (p[at + 1, own, :] - p[at - 1, own, :])),
            STEP_DT * (0.5 * (wide[9 : 9 + span_y] - wide[7 : 7 + span_y])),
            STEP_DT * (0.5 * (up - down)),
        )

    p = run([(whole, ITERS - 1)])
    cost = jnp.zeros((span_y, depth), F32)
    for x in range(span_x):
        moves = correction(p, x)
        for c in range(3):
            updated = q_ref[c, x].astype(F32) - moves[c]
            new_ref[c, x] = updated.astype(BF16)
            mismatch = updated - t_ref[c, x].astype(F32)
            cost = cost + mismatch * mismatch
            seed[c, x] = 2.0 * mismatch
    cost_ref[...] = cost[0:8] + sum((cost[k : k + 8] for k in range(8, span_y, 8)), jnp.zeros((8, depth), F32))

    other = pa if p is pb else pb

    def second_source(x, carry):
        centre = p[x + 2, rows, :]
        to_high = jnp.where(x + 1 < total_x, 0.25, 0.0)
        to_low = jnp.where(x > 0, 0.25, 0.0)
        wide = to_high * (p[x + 4, rows, :] - centre) - to_low * (centre - p[x, rows, :])
        row = lax.broadcasted_iota(jnp.int32, centre.shape, 0)
        lane = lax.broadcasted_iota(jnp.int32, centre.shape, 1)
        wide = wide + 0.25 * (
            jnp.where(row < total_y - 1, p[x + 2, 10 : 10 + total_y, :] - centre, 0.0)
            - jnp.where(row > 0, centre - p[x + 2, 6 : 6 + total_y, :], 0.0)
        )
        up, down = lane_shifts(centre, 2)
        wide = wide + 0.25 * (
            jnp.where(lane < depth - 1, up - centre, 0.0) - jnp.where(lane > 0, centre - down, 0.0)
        )
        value = (2.0 * unit) * (div[x + 1, rows, :] - STEP_DT * wide - div_t[x])
        source[x] = value
        other[x + 2, rows, :] = -value
        return carry

    lax.fori_loop(0, total_x, second_source, 0, unroll=4)
    p = run(windows(), start=0 if p is pb else 1)
    for x in range(span_x):
        moves = correction(p, x)
        for c in range(3):
            grad_ref[c, x] = (STEP_DT * (seed[c, x] - moves[c])).astype(BF16)


def backward_kernel(
    grad_ref, feat_ref, one_ref, two_ref, w_out, w_mid, cost_ref,
    sum_ref,
    stage, acc_mid, acc_in, acc_out, acc_b, w_out_t, w_mid_t,
):
    planes, span_y, depth = grad_ref.shape[1:]
    lines = planes * span_y
    units = one_ref.shape[0]
    i = pl.program_id(0)

    @pl.when(i == 0)
    def _():
        stage[...] = jnp.zeros_like(stage)
        acc_mid[...] = jnp.zeros_like(acc_mid)
        acc_in[...] = jnp.zeros_like(acc_in)
        acc_out[...] = jnp.zeros_like(acc_out)
        acc_b[...] = jnp.zeros_like(acc_b)
        out = jnp.concatenate([w_out[...].astype(F32), jnp.zeros((13, units), F32)], 0)
        w_out_t[...] = out.T.astype(BF16)
        w_mid_t[...] = w_mid[...].astype(F32).T.astype(BF16)

    for k in range(planes):
        for c in range(3):
            stage[pl.ds(16 * span_y * k + c, span_y, stride=16), :] = grad_ref[c, k].astype(F32)
    grad = jnp.concatenate([stage[16 * y : 16 * y + 16, :].astype(BF16) for y in range(lines)], 1)
    bias = stage[0:8, :]
    for y in range(1, lines):
        bias = bias + stage[16 * y : 16 * y + 8, :]
    acc_b[...] += bias
    hidden_one, hidden_two = one_ref[...], two_ref[...]
    acc_out[...] += dot_nt(grad, hidden_two)
    two_value = hidden_two.astype(F32)
    delta_two = (dot(w_out_t[...], grad) * (1.0 - two_value * two_value)).astype(BF16)
    ones = jnp.ones((16, hidden_one.shape[1]), BF16)
    acc_mid[...] += dot_nt(jnp.concatenate([hidden_one, ones], 0), delta_two)
    one_value = hidden_one.astype(F32)
    delta_one = (dot(w_mid_t[...], delta_two) * (1.0 - one_value * one_value)).astype(BF16)
    acc_in[...] += dot_nt(feat_ref[...], delta_one)

    @pl.when(i == pl.num_programs(0) - 1)
    def _():
        sum_ref[...] = jnp.zeros_like(sum_ref)
        sum_ref[0:units, :] = acc_mid[0:units, :]
        sum_ref[units : units + 13, :] = acc_in[0:13, :]
        sum_ref[units + 13 : units + 14, :] = acc_mid[units : units + 1, :]
        sum_ref[units + 14 : units + 17, :] = acc_out[0:3, :]
        lane = lax.broadcasted_iota(jnp.int32, (1, units), 1)
        row = jnp.where(lane == 3, jnp.sum(cost_ref[...]), 0.0)
        for c in range(3):
            row = row + jnp.where(lane == c, jnp.sum(acc_b[c : c + 1, :]), 0.0)
        sum_ref[units + 17 : units + 18, :] = row


def finish_kernel(spot_of, entry_total, cell_total, *refs):
    n = len(refs) - 8
    pieces = refs[:n]
    loss_ref, in_ref, b_in_ref, mid_ref, b_mid_ref, out_ref, b_out_ref, whole = refs[n:]
    units = mid_ref.shape[0]
    feats = in_ref.shape[0]
    size = pieces[0].shape[0]
    for ref, spot in zip(pieces, spot_of()):
        whole[pl.ds(pl.multiple_of(spot * size, 8), size), :] = ref[...]
    mid = whole[0:units, :]
    small = whole[units : units + 32, :]
    row = lax.broadcasted_iota(jnp.int32, small.shape, 0)
    lane = lax.broadcasted_iota(jnp.int32, small.shape, 1)
    counted = (row < feats + 5) | ((row == feats + 5) & (lane < 3))
    squares = jnp.sum(mid * mid) + jnp.sum(jnp.where(counted, small * small, 0.0))
    scale = jnp.full((1, 1), 1.0, F32) / jnp.sqrt(jnp.full((1, 1), 1.0, F32) * squares / entry_total + EPSILON_RMS)
    small = small * scale
    mid_ref[...] = (mid * scale).T
    in_ref[...] = small[0:feats]
    b_in_ref[...] = small[feats : feats + 1]
    b_mid_ref[...] = small[feats + 1 : feats + 2]
    out_ref[...] = small[feats + 2 : feats + 5]
    b_out_ref[...] = small[feats + 5 : feats + 6, 0:3]
    loss_ref[...] = whole[units + feats + 5 : units + feats + 6, 3:4] / cell_total


def is_power(count):
    return count & (count - 1) == 0


def partner(index, step, count):
    return index ^ step if is_power(count) else (index + step) % count


def pair_list(count, offset):
    pairs = []
    for low in range(offset, count - 1, 2):
        pairs += [(low, low + 1), (low + 1, low)]
    return pairs


def face_plan(n_x, n_y):
    plan = []
    for dim, count in ((0, n_x), (1, n_y)):
        if count > 1:
            plan.append((dim, 0))
        if count > 2:
            plan.append((dim, 1))
    return tuple(plan)


def swap(values, axis, step):
    count = lax.axis_size(axis)
    return lax.ppermute(values, axis, [(i, partner(i, step, count)) for i in range(count)])


def swap_both(values, step_x, step_y):
    n_x, n_y = lax.axis_size("gx"), lax.axis_size("gy")
    pairs = [
        (i * n_y + j, partner(i, step_x, n_x) * n_y + partner(j, step_y, n_y)) for i in range(n_x) for j in range(n_y)
    ]
    return lax.ppermute(values, ("gx", "gy"), pairs)


def gather_doubling(values, order):
    held = {(0, 0): values}
    for axis, bit in order:
        for (sx, sy), block in list(held.items()):
            key = (sx ^ bit, sy) if axis == "gx" else (sx, sy ^ bit)
            held[key] = swap(block, axis, bit)
    return held


def bits_of(axis, count):
    return [(axis, 1 << k) for k in reversed(range(count.bit_length() - 1))]


def on_device(
    velocity,
    target,
    weight_in,
    bias_in,
    weight_mid,
    bias_mid,
    weight_out,
    bias_out,
    thrust_coef,
    tile_cells,
    tile_turbine,
    tile_weight,
):
    v, t = velocity[0], target[0]
    _, span_x, span_y, depth = v.shape
    units, feats = weight_in.shape
    cells = span_x * span_y * depth
    turbines = thrust_coef.shape[0]
    n_case, n_x, n_y = lax.axis_size("case"), lax.axis_size("gx"), lax.axis_size("gy")
    ix, iy = lax.axis_index("gx"), lax.axis_index("gy")
    plan = face_plan(n_x, n_y)
    shape_of = jax.ShapeDtypeStruct

    start_kernel.plan = plan
    started = pl.pallas_call(
        start_kernel,
        name="start",
        out_shape=tuple(shape_of((6, span_y if d == 0 else span_x, depth), BF16) for d, _ in plan)
        + (shape_of((8, turbines), F32),),
        in_specs=[vspec(), sspec(), vspec(), vspec(), vspec()],
        out_specs=tuple(vspec() for _ in range(len(plan) + 1)),
        compiler_params=pltpu.CompilerParams(vmem_limit_bytes=LIMIT),
    )(tile_cells, tile_turbine, tile_weight, v, t)
    disk = started[-1]
    faces = []
    for face, (dim, parity) in zip(started[:-1], plan):
        axis, count = (("gx", n_x), ("gy", n_y))[dim]
        faces.append(lax.ppermute(face, axis, pair_list(count, parity)))
    if n_y > 1 and is_power(n_y) and is_power(n_x):
        disk = disk + swap(disk, "gy", 1)
        disks = [disk] + [
            swap_both(disk, a, b) for a in range(n_x) for b in range(0, n_y, 2) if (a, b) != (0, 0)
        ]
    else:
        disks = [swap_both(disk, a, b) for a in range(n_x) for b in range(n_y)]

    whole = lambda shape: pl.BlockSpec(shape, lambda i: (0,) * len(shape))
    planes = 2 if span_x % 2 == 0 else 1
    chunk = planes * span_y * depth
    face_shape = [f.shape for f in faces]
    hidden_one, hidden_two, features, closure = pl.pallas_call(
        functools.partial(forward_kernel, plan, len(faces)),
        name="closure_forward",
        grid=(span_x // planes,),
        out_shape=(
            shape_of((units, cells), BF16),
            shape_of((units, cells), BF16),
            shape_of((16, cells), BF16),
            shape_of((3, span_x, span_y, depth), F32),
        ),
        in_specs=[whole(s) for s in face_shape]
        + [
            whole(v.shape),
            whole((feats, units)),
            whole((1, units)),
            whole(weight_mid.shape),
            whole((1, units)),
            whole(weight_out.shape),
            sspec(),
        ],
        out_specs=(
            pl.BlockSpec((units, chunk), lambda i: (0, i)),
            pl.BlockSpec((units, chunk), lambda i: (0, i)),
            pl.BlockSpec((16, chunk), lambda i: (0, i)),
            pl.BlockSpec((3, planes, span_y, depth), lambda i: (0, i, 0, 0)),
        ),
        scratch_shapes=[
            VMEM((3, span_x + 2, span_y + 16, depth), F32),
            VMEM((16 * planes * span_y, depth), F32),
            VMEM((8 * planes * span_y, depth), F32),
            VMEM((units, 16), BF16),
            VMEM((units, 8), F32),
        ],
        compiler_params=pltpu.CompilerParams(vmem_limit_bytes=LIMIT),
    )(*faces, v, weight_in.T, bias_in.reshape(1, units), weight_mid, bias_mid.reshape(1, units), weight_out, bias_out)

    message = shape_of((span_x + 2, span_y, depth), F32)
    prov, first, second = pl.pallas_call(
        functools.partial(provisional_kernel, plan, len(faces), len(disks)),
        name="provisional",
        out_shape=(shape_of(v.shape, BF16), message, message),
        in_specs=[sspec()] + [vspec() for _ in range(len(faces) + len(disks) + 6)],
        out_specs=(vspec(), vspec(), vspec()),
        scratch_shapes=[
            VMEM((3, span_x + 2, span_y + 16, depth), F32),
            VMEM((span_x * span_y, depth), F32),
            VMEM((3, span_x + 2, span_y + 16, depth), F32),
        ],
        compiler_params=pltpu.CompilerParams(vmem_limit_bytes=LIMIT),
    )(tile_turbine, *faces, *disks, tile_cells, tile_weight, thrust_coef.reshape(1, turbines), v, t, closure)

    if is_power(n_x) and is_power(n_y):
        x_bits, y_bits = bits_of("gx", n_x), bits_of("gy", n_y)
        firsts = gather_doubling(first, x_bits + y_bits)
        seconds = gather_doubling(second, y_bits[:-1] + x_bits + y_bits[-1:])
    else:
        steps = [(a, b) for a in range(n_x) for b in range(n_y)]
        firsts = {s: swap_both(first, *s) for s in steps}
        seconds = {s: swap_both(second, *s) for s in steps}
    offsets = sorted(firsts)
    total_x, total_y = n_x * span_x, n_y * span_y
    new, force_field, cost = pl.pallas_call(
        functools.partial(solve_kernel, tuple(offsets), n_x, n_y),
        name="solve",
        out_shape=(shape_of(v.shape, BF16), shape_of(v.shape, BF16), shape_of((8, depth), F32)),
        in_specs=[vspec() for _ in range(2 * len(offsets) + 2)],
        out_specs=(vspec(), vspec(), vspec()),
        scratch_shapes=[
            VMEM((total_x + 2, total_y + 16, depth), F32),
            VMEM((total_x, total_y, depth), F32),
            VMEM((total_x, total_y, depth), F32),
            VMEM((total_x + 4, total_y + 16, depth), F32),
            VMEM((total_x + 4, total_y + 16, depth), F32),
            VMEM((3, span_x, span_y, depth), F32),
        ],
        compiler_params=pltpu.CompilerParams(vmem_limit_bytes=LIMIT),
    )(*[firsts[o] for o in offsets], *[seconds[o] for o in offsets], prov, t)

    n_pieces = n_x * n_y
    total_rows = -(-(units + 32) // (8 * n_pieces)) * 8 * n_pieces
    sums = pl.pallas_call(
        backward_kernel,
        name="closure_backward",
        grid=(span_x // planes,),
        out_shape=shape_of((total_rows, units), F32),
        in_specs=[
            pl.BlockSpec((3, planes, span_y, depth), lambda i: (0, i, 0, 0)),
            pl.BlockSpec((16, chunk), lambda i: (0, i)),
            pl.BlockSpec((units, chunk), lambda i: (0, i)),
            pl.BlockSpec((units, chunk), lambda i: (0, i)),
            whole(weight_out.shape),
            whole(weight_mid.shape),
            whole((8, depth)),
        ],
        out_specs=whole((total_rows, units)),
        scratch_shapes=[
            VMEM((16 * planes * span_y, depth), F32),
            VMEM((units + 16, units), F32),
            VMEM((16, units), F32),
            VMEM((16, units), F32),
            VMEM((8, depth), F32),
            VMEM((units, 16), BF16),
            VMEM((units, units), BF16),
        ],
        compiler_params=pltpu.CompilerParams(vmem_limit_bytes=LIMIT),
    )(force_field, features, hidden_one, hidden_two, weight_out, weight_mid, cost)

    if n_y > 1 and is_power(n_x) and is_power(n_y) and is_power(n_case):
        group = n_pieces // 2
        size = total_rows // n_pieces
        sums = sums + swap(sums, "gy", 1)
        mine = lax.dynamic_slice_in_dim(sums, (iy & 1) * (group * size), group * size, 0)
        steps = [(a, b) for a in range(n_x) for b in range(0, n_y, 2)]
        spot = lambda a, b: (ix ^ a) * (n_y // 2) + ((iy ^ b) >> 1)
        cut = lambda s: lax.dynamic_slice_in_dim(mine, spot(*s) * size, size, 0)
        piece = cut((0, 0))
        for s in steps[1:]:
            piece = piece + swap_both(cut(s), *s)
        others = [swap(piece, "case", m) for m in range(1, n_case)]
        for other in others:
            piece = piece + other
        here = [piece] + [swap_both(piece, *s) for s in steps[1:]]
        there = [swap(p, "gy", 1) for p in here]
        pieces = here + there

        def spot_of():
            jx, jy = lax.axis_index("gx"), lax.axis_index("gy")
            base = [(jx ^ a) * (n_y // 2) + ((jy ^ b) >> 1) for a, b in steps]
            return [(jy & 1) * group + k for k in base] + [(1 - (jy & 1)) * group + k for k in base]

    else:
        pieces = [lax.psum(sums, ("case", "gx", "gy"))]
        spot_of = lambda: [0]

    entry_total = units * feats + units + units * units + units + 3 * units + 3
    cell_total = 3 * cells * n_case * n_x * n_y
    loss, s_in, sb_in, s_mid, sb_mid, s_out, sb_out = pl.pallas_call(
        functools.partial(finish_kernel, spot_of, entry_total, cell_total),
        name="finish",
        out_shape=(
            shape_of((1, 1), F32),
            shape_of((feats, units), F32),
            shape_of((1, units), F32),
            shape_of((units, units), F32),
            shape_of((1, units), F32),
            shape_of((3, units), F32),
            shape_of((1, 3), F32),
        ),
        in_specs=[vspec() for _ in pieces],
        out_specs=tuple(vspec() for _ in range(7)),
        scratch_shapes=[VMEM((total_rows, units), F32)],
        compiler_params=pltpu.CompilerParams(vmem_limit_bytes=LIMIT),
    )(*pieces)
    return (
        new[None],
        loss.reshape(()),
        s_in.T,
        sb_in.reshape(units),
        s_mid,
        sb_mid.reshape(units),
        s_out,
        sb_out.reshape(3),
        force_field[None],
    )


def solution(mesh):
    placed = (
        P("case", None, "gx", "gy", None),
        P("case", None, "gx", "gy", None),
        P(),
        P(),
        P(),
        P(),
        P(),
        P(),
        P(),
        P(("gx", "gy"), None),
        P(("gx", "gy")),
        P(("gx", "gy"), None),
    )
    field = P("case", None, "gx", "gy", None)
    return jax.shard_map(
        on_device,
        mesh=mesh,
        in_specs=placed,
        out_specs=(field, P(), P(), P(), P(), P(), P(), P(), field),
        check_vma=False,
    )
```

```python
import functools

import jax
import jax.numpy as jnp
import numpy as np
from jax import lax
from jax.experimental import pallas as pl
from jax.experimental.pallas import tpu as pltpu
from jax.sharding import PartitionSpec as P


ITERS = 20
INFLOW = 1.0
STEP_DT = 0.4
VISCOSITY = 0.1
EPSILON_RMS = 1e-06

F32 = jnp.float32
BF16 = jnp.bfloat16
VMEM = pltpu.VMEM
LIMIT = 58 * 1024 * 1024


def parity_of(dim):
    return lax.axis_index(("gx", "gy")[dim]) & 1


def vspec():
    return pl.BlockSpec(memory_space=pltpu.VMEM)


def sspec():
    return pl.BlockSpec(memory_space=pltpu.SMEM)


def dot(a, b):
    return lax.dot_general(a, b, (((1,), (0,)), ((), ())), preferred_element_type=F32)


def dot_nt(a, b):
    return lax.dot_general(a, b, (((1,), (1,)), ((), ())), preferred_element_type=F32)


def dot_full(a, b):
    return lax.dot_general(
        a, b, (((1,), (0,)), ((), ())), precision=lax.Precision.HIGHEST, preferred_element_type=F32
    )


def depth_basis(depth):
    mode = np.arange(1, depth + 1, dtype=np.float64)
    basis = np.sqrt(2.0 / (depth + 1)) * np.sin(np.pi * np.outer(mode, mode) / (depth + 1))
    slope = 0.5 * (np.eye(depth, k=-1) - np.eye(depth, k=1))
    matrices = np.stack([basis, basis @ slope, basis @ slope @ slope @ basis])
    return matrices.astype(np.float32), (2.0 * np.cos(np.pi * mode / (depth + 1))).astype(np.float32)[None]


def lane_shifts(values, step=1):
    depth = values.shape[-1]
    axis = values.ndim - 1
    lane = lax.broadcasted_iota(jnp.int32, values.shape, axis)
    up = jnp.where(lane < depth - step, pltpu.roll(values, depth - step, axis), 0.0)
    down = jnp.where(lane >= step, pltpu.roll(values, step, axis), 0.0)
    return up, down


def start_kernel(cells_ref, turbine_ref, weight_ref, v_ref, t_ref, *outs):
    n_x_sends = (len(outs) - 1) // 2 if False else None
    del n_x_sends
    face_refs, disk_ref = outs[:-1], outs[-1]
    span_x, span_y, depth = v_ref.shape[1:]
    for ref, (dim, high_parity) in zip(face_refs, start_kernel.plan):
        take_high = parity_of(dim) == high_parity
        for part, source in enumerate((v_ref, t_ref)):
            for c in range(3):
                if dim == 0:
                    high, low = source[c, span_x - 1], source[c, 0]
                    ref[3 * part + c] = jnp.where(take_high, high.astype(F32), low.astype(F32)).astype(BF16)
                else:
                    for x in range(span_x):
                        plane = source[c, x].astype(F32)
                        row = jnp.where(take_high, plane[span_y - 1 : span_y], plane[0:1])
                        ref[3 * part + c, x : x + 1, :] = row.astype(BF16)
    rows = span_x * span_y
    tiles, width = cells_ref.shape
    stream = v_ref[0].astype(F32).reshape(rows, depth).T.astype(BF16)
    pick = []
    for r in range(tiles):
        cell_row = cells_ref[r : r + 1, :] // depth
        spot = lax.broadcasted_iota(jnp.int32, (rows, width), 0)
        pick.append((spot == cell_row).astype(F32).astype(BF16))
    found = dot(stream, jnp.concatenate(pick, 1))
    turbines = disk_ref.shape[1]
    lane = lax.broadcasted_iota(jnp.int32, (1, turbines), 1)
    total = jnp.zeros((1, turbines), F32)
    area = jnp.zeros((1, turbines), F32)
    spot = lax.broadcasted_iota(jnp.int32, (depth, width), 0)
    for r in range(tiles):
        cell_lane = cells_ref[r : r + 1, :] % depth
        values = jnp.sum(jnp.where(spot == cell_lane, found[:, r * width : (r + 1) * width], 0.0), 0, keepdims=True)
        weight = weight_ref[r : r + 1, :]
        weighted = jnp.sum(weight * (values + INFLOW), 1, keepdims=True)
        summed = jnp.sum(weight, 1, keepdims=True)
        mine = lane == turbine_ref[r]
        total = total + jnp.where(mine, weighted, 0.0)
        area = area + jnp.where(mine, summed, 0.0)
    disk_ref[...] = jnp.zeros_like(disk_ref)
    disk_ref[0:1, :] = total
    disk_ref[1:2, :] = area


def fill_padded(pad, source, first, faces, plan):
    span_x, span_y = source.shape[1], source.shape[2]
    depth = source.shape[3]
    zero_plane = jnp.zeros((span_y, depth), F32)
    zero_rows = jnp.zeros((span_x, depth), F32)
    for c in range(3):
        for x in range(span_x):
            pad[c, 1 + x, 8 : 8 + span_y, :] = source[c, x].astype(F32)
        low = {0: zero_plane, 1: zero_rows}
        high = {0: zero_plane, 1: zero_rows}
        for ref, (dim, high_parity) in zip(faces, plan):
            got = ref[first + c].astype(F32)
            is_high = parity_of(dim) == high_parity
            high[dim] = jnp.where(is_high, got, high[dim])
            low[dim] = jnp.where(is_high, low[dim], got)
        pad[c, 0, 8 : 8 + span_y, :] = low[0]
        pad[c, 1 + span_x, 8 : 8 + span_y, :] = high[0]
        for x in range(span_x):
            pad[c, 1 + x, 7:8, :] = low[1][x : x + 1]
            pad[c, 1 + x, 8 + span_y : 9 + span_y, :] = high[1][x : x + 1]


def forward_kernel(plan, n_faces, *refs):
    faces = refs[:n_faces]
    (
        v_ref, w_in_t, b_in, w_mid, b_mid, w_out, b_out,
        one_ref, two_ref, feat_ref, closure_ref,
        pad, stage, stage_out, w_in, b_column,
    ) = refs[n_faces:]
    span_y, depth = v_ref.shape[2], v_ref.shape[3]
    planes = closure_ref.shape[1]
    lines = planes * span_y
    i = pl.program_id(0)

    @pl.when(i == 0)
    def _():
        fill_padded(pad, v_ref, 0, faces, plan)
        channel = lax.broadcasted_iota(jnp.int32, stage.shape, 0) % 16
        stage[...] = jnp.where((channel >= 12) & (channel < 15), 1.0, 0.0)
        bias = b_in[...]
        high = bias.astype(BF16).astype(F32)
        rest = bias - high
        middle = rest.astype(BF16).astype(F32)
        rows = jnp.concatenate([w_in_t[...].astype(F32), high, middle, rest - middle, jnp.zeros_like(bias)], 0)
        w_in[...] = rows.T.astype(BF16)
        b_column[...] = jnp.broadcast_to(b_mid[...], (8, bias.shape[1])).T

    for k in range(planes):
        x = i * planes + k
        own = slice(8, 8 + span_y)

        def put(channel, value):
            stage[pl.ds(16 * span_y * k + channel, span_y, stride=16), :] = value

        for c in range(3):
            centre = pad[c, x + 1, own, :]
            put(c, 0.5 * (pad[c, x + 2, own, :] - pad[c, x, own, :]))
            put(3 + c, 0.5 * (pad[c, x + 1, 9 : 9 + span_y, :] - pad[c, x + 1, 7 : 7 + span_y, :]))
            up, down = lane_shifts(centre)
            put(6 + c, 0.5 * (up - down))
            put(9 + c, centre)
    features = jnp.concatenate([stage[16 * y : 16 * y + 16, :].astype(BF16) for y in range(lines)], 1)
    feat_ref[...] = features
    hidden_one = jnp.tanh(dot(w_in[...], features)).astype(BF16)
    one_ref[...] = hidden_one
    hidden_two = jnp.tanh(dot(w_mid[...], hidden_one) + b_column[:, 0:1]).astype(BF16)
    two_ref[...] = hidden_two
    out = dot(w_out[...], hidden_two)
    for y in range(lines):
        stage_out[8 * y : 8 * y + 3, :] = out[:, y * depth : (y + 1) * depth]
    for k in range(planes):
        for c in range(3):
            closure_ref[c, k] = stage_out[pl.ds(8 * span_y * k + c, span_y, stride=8), :] + b_out[c]


def provisional_kernel(plan, n_faces, n_disks, turbine_ref, *refs):
    faces = refs[:n_faces]
    disks = refs[n_faces : n_faces + n_disks]
    (cells_ref, weight_ref, coef_ref, v_ref, t_ref, closure_ref, basis_ref, prov_ref, first_out, second_out, pad, force, qpad, first_ref, second_ref) = refs[
        n_faces + n_disks :
    ]
    span_x, span_y, depth = v_ref.shape[1:]
    rows = span_x * span_y
    tiles, width = cells_ref.shape
    half = span_x // 2
    sums = disks[0][...]
    for extra in disks[1:]:
        sums = sums + extra[...]
    speed = sums[0:1, :] / jnp.maximum(sums[1:2, :], 1.0)
    thrust = -0.5 * coef_ref[...] * speed * jnp.abs(speed)
    lane = lax.broadcasted_iota(jnp.int32, thrust.shape, 1)
    spot_row = lax.broadcasted_iota(jnp.int32, (rows, width), 0)
    spot_lane = lax.broadcasted_iota(jnp.int32, (depth, width), 0)
    pick, spread = [], []
    for r in range(tiles):
        row_thrust = jnp.sum(jnp.where(lane == turbine_ref[r], thrust, 0.0), 1, keepdims=True)
        strength = weight_ref[r : r + 1, :] * row_thrust
        cell = cells_ref[r : r + 1, :]
        pick.append((spot_row == cell // depth).astype(F32).astype(BF16))
        spread.append(jnp.where(spot_lane == cell % depth, strength, 0.0))
    pick = jnp.concatenate(pick, 1)
    spread = jnp.concatenate(spread, 1)
    hi = spread.astype(BF16)
    rest = spread - hi.astype(F32)
    mid = rest.astype(BF16)
    low = (rest - mid.astype(F32)).astype(BF16)
    force[...] = dot_nt(pick, hi) + (dot_nt(pick, mid) + dot_nt(pick, low))

    fill_padded(pad, t_ref, 3, faces, plan)
    for x in range(span_x):
        up, down = lane_shifts(pad[2, x + 1, 8 : 8 + span_y, :])
        value = (
            0.5 * (pad[0, x + 2, 8 : 8 + span_y, :] - pad[0, x, 8 : 8 + span_y, :])
            + 0.5 * (pad[1, x + 1, 9 : 9 + span_y, :] - pad[1, x + 1, 7 : 7 + span_y, :])
            + 0.5 * (up - down)
        )
        where_to = first_ref if x < half else second_ref
        where_to[half + x % half] = value

    fill_padded(pad, v_ref, 0, faces, plan)
    qpad[...] = jnp.zeros_like(qpad)
    for x in range(span_x):
        centre = [pad[c, x + 1, 8 : 8 + span_y, :] for c in range(3)]
        for c in range(3):
            xp, xm = pad[c, x + 2, 8 : 8 + span_y, :], pad[c, x, 8 : 8 + span_y, :]
            yp, ym = pad[c, x + 1, 9 : 9 + span_y, :], pad[c, x + 1, 7 : 7 + span_y, :]
            zp, zm = lane_shifts(centre[c])
            laplace = (xp + xm) + yp + ym + zp + zm - 6.0 * centre[c]
            advect = (
                (centre[0] + INFLOW) * (0.5 * (xp - xm)) + centre[1] * (0.5 * (yp - ym)) + centre[2] * (0.5 * (zp - zm))
            )
            tendency = VISCOSITY * laplace - advect + closure_ref[c, x]
            if c == 0:
                tendency = tendency + force[x * span_y : (x + 1) * span_y, :]
            value = (centre[c] + STEP_DT * tendency).astype(BF16)
            prov_ref[c, x] = value
            qpad[c, 1 + x, 8 : 8 + span_y, :] = value.astype(F32)
    for x in range(span_x):
        up, down = lane_shifts(qpad[2, x + 1, 8 : 8 + span_y, :])
        value = (
            0.5 * (qpad[0, x + 2, 8 : 8 + span_y, :] - qpad[0, x, 8 : 8 + span_y, :])
            + 0.5 * (qpad[1, x + 1, 9 : 9 + span_y, :] - qpad[1, x + 1, 7 : 7 + span_y, :])
            + 0.5 * (up - down)
        )
        where_to = first_ref if x < half else second_ref
        where_to[x % half] = value
        second_ref[2 * half, x : x + 1, :] = 0.5 * qpad[1, 1 + x, 8:9, :]
        second_ref[2 * half + 1, x : x + 1, :] = -0.5 * qpad[1, 1 + x, 7 + span_y : 8 + span_y, :]
    first_ref[2 * half] = 0.5 * qpad[0, 1, 8 : 8 + span_y, :]
    first_ref[2 * half + 1] = -0.5 * qpad[0, span_x, 8 : 8 + span_y, :]
    for scratch, out in ((first_ref, first_out), (second_ref, second_out)):
        out[...] = dot_full(scratch[...].reshape(-1, depth), basis_ref[0]).reshape(out.shape)


def solve_kernel(offsets, n_x, n_y, *refs):
    n = len(offsets)
    firsts, seconds = refs[:n], refs[n : 2 * n]
    q_ref, t_ref, basis_ref, modes_ref, new_ref, grad_ref, cost_ref, div, div_t, source, pa, pb, seed, moved, twice = refs[2 * n :]
    span_x, span_y, depth = q_ref.shape[1:]
    total_x, total_y = source.shape[0], source.shape[1]
    half = span_x // 2
    rows = slice(8, 8 + total_y)
    ix, iy = lax.axis_index("gx"), lax.axis_index("gy")

    pa[...] = jnp.zeros_like(pa)
    pb[...] = jnp.zeros_like(pb)
    spots = []
    for mx, my in offsets:
        spots.append((partner(ix, mx, total_x // span_x) * span_x, pl.multiple_of(partner(iy, my, total_y // span_y) * span_y, span_y)))
    for k, (x0, y0) in enumerate(spots):
        for ref, base in ((firsts[k], 0), (seconds[k], half)):
            for x in range(half):
                div[x0 + base + x + 1, pl.ds(pl.multiple_of(y0 + 8, 8), span_y), :] = ref[x]
                div_t[x0 + base + x, pl.ds(y0, span_y), :] = ref[half + x]
    for k, (x0, y0) in enumerate(spots):
        own = pl.ds(pl.multiple_of(y0 + 8, 8), span_y)
        div[x0, own, :] = div[x0, own, :] + firsts[k][2 * half]
        div[x0 + span_x + 1, own, :] = div[x0 + span_x + 1, own, :] + firsts[k][2 * half + 1]
        for x in range(span_x):
            below = pl.ds(y0 + 7, 1)
            above = pl.ds(y0 + 8 + span_y, 1)
            div[x0 + x + 1, below, :] = div[x0 + x + 1, below, :] + seconds[k][2 * half, x : x + 1, :]
            div[x0 + x + 1, above, :] = div[x0 + x + 1, above, :] + seconds[k][2 * half + 1, x : x + 1, :]

    unit = 1.0 / (6.0 * STEP_DT)

    def first_source(x, carry):
        value = div[x + 1, rows, :] * unit
        source[x] = value
        pa[x + 2, rows, :] = -value
        return carry

    lax.fori_loop(0, total_x, first_source, 0, unroll=4)

    def sweep(src, dst, x_start, x_count, y_start, y_count):
        own = pl.ds(y_start + 8, y_count)
        mode = modes_ref[...]
        group = x_count if x_count <= 32 else 32

        def planes(i, carry):
            base = x_start + i * group
            loaded = {}

            def plane(k):
                if k not in loaded:
                    loaded[k] = src[base + k, own, :]
                return loaded[k]

            for k in range(group):
                centre = plane(k + 2)
                across = plane(k + 1) + plane(k + 3)
                beside = src[base + k + 2, pl.ds(y_start + 9, y_count), :] + src[base + k + 2, pl.ds(y_start + 7, y_count), :]
                around = (across + beside) + mode * centre
                dst[base + k + 2, own, :] = around * (1.0 / 6.0) - source[base + k, pl.ds(y_start, y_count), :]
                loaded.pop(k + 1)
            return carry

        if x_count == group:
            planes(0, 0)
        else:
            lax.fori_loop(0, x_count // group, planes, 0)

    def run(stages, start=0):
        buffers, now = (pa, pb), start
        for window, count in stages:

            def two(k, carry, now=now, window=window):
                sweep(buffers[now], buffers[1 - now], *window)
                sweep(buffers[1 - now], buffers[now], *window)
                return carry

            if count // 2:
                lax.fori_loop(0, count // 2, two, 0)
            if count % 2:
                sweep(buffers[now], buffers[1 - now], *window)
                now = 1 - now
        return buffers[now]

    whole = (0, total_x, 0, total_y)

    def windows():
        stages = []
        left = ITERS - 1
        for k in range(left):
            margin = -(-(left - k) // 8) * 8
            x_count = min(total_x, span_x + margin * min(n_x - 1, 2))
            y_count = min(total_y, span_y + margin * min(n_y - 1, 2))
            key = (margin, x_count, y_count)
            if stages and (stages[-1][0][1:] == key[1:]):
                stages[-1][1] += 1
            else:
                stages.append([key, 1])
        result = []
        for (margin, x_count, y_count), count in stages:
            x_start = 0 if x_count == total_x else jnp.clip(ix * span_x - margin, 0, total_x - x_count)
            y_start = 0
            if y_count != total_y:
                y_start = pl.multiple_of(jnp.clip(iy * span_y - margin, 0, total_y - y_count), 8)
            result.append(((x_start, x_count, y_start, y_count), count))
        return result

    def correction(p):
        y0 = pl.multiple_of(iy * span_y, 8)
        own = pl.ds(pl.multiple_of(y0 + 8, 8), span_y)
        for x in range(span_x):
            at = ix * span_x + x + 2
            wide = p[at, pl.ds(y0, span_y + 16), :]
            lines = slice(x * span_y, (x + 1) * span_y)
            moved[0, lines, :] = (0.5 * STEP_DT) * (p[at + 1, own, :] - p[at - 1, own, :])
            moved[1, lines, :] = (0.5 * STEP_DT) * (wide[9 : 9 + span_y] - wide[7 : 7 + span_y])
            moved[2, lines, :] = STEP_DT * wide[8 : 8 + span_y]
        for c in range(3):
            moved[c] = dot_full(moved[c], basis_ref[0 if c < 2 else 1])

    p = run([(whole, ITERS - 1)])
    cost = jnp.zeros((span_y, depth), F32)
    correction(p)
    for x in range(span_x):
        for c in range(3):
            updated = q_ref[c, x].astype(F32) - moved[c, x * span_y : (x + 1) * span_y, :]
            new_ref[c, x] = updated.astype(BF16)
            mismatch = updated - t_ref[c, x].astype(F32)
            cost = cost + mismatch * mismatch
            seed[c, x] = 2.0 * mismatch
    cost_ref[...] = cost[0:8] + sum((cost[k : k + 8] for k in range(8, span_y, 8)), jnp.zeros((8, depth), F32))

    other = pa if p is pb else pb
    together = 8

    def vertical(i, carry):
        some = pl.ds(i * together, together)
        values = p[pl.ds(i * together + 2, together), rows, :].reshape(-1, depth)
        twice[some] = dot_full(values, basis_ref[2]).reshape(together, total_y, depth)
        return carry

    lax.fori_loop(0, total_x // together, vertical, 0)

    def second_source(x, carry):
        centre = p[x + 2, rows, :]
        to_high = jnp.where(x + 1 < total_x, 0.25, 0.0)
        to_low = jnp.where(x > 0, 0.25, 0.0)
        wide = to_high * (p[x + 4, rows, :] - centre) - to_low * (centre - p[x, rows, :])
        row = lax.broadcasted_iota(jnp.int32, centre.shape, 0)
        wide = wide + 0.25 * (
            jnp.where(row < total_y - 1, p[x + 2, 10 : 10 + total_y, :] - centre, 0.0)
            - jnp.where(row > 0, centre - p[x + 2, 6 : 6 + total_y, :], 0.0)
        )
        wide = wide + twice[x]
        value = (2.0 * unit) * (div[x + 1, rows, :] - STEP_DT * wide - div_t[x])
        source[x] = value
        other[x + 2, rows, :] = -value
        return carry

    lax.fori_loop(0, total_x, second_source, 0, unroll=4)
    p = run(windows(), start=0 if p is pb else 1)
    correction(p)
    for x in range(span_x):
        for c in range(3):
            grad_ref[c, x] = (STEP_DT * (seed[c, x] - moved[c, x * span_y : (x + 1) * span_y, :])).astype(BF16)


def backward_kernel(
    grad_ref, feat_ref, one_ref, two_ref, w_out, w_mid, cost_ref,
    sum_ref,
    stage, acc_mid, acc_in, acc_out, acc_b, w_out_t, w_mid_t,
):
    planes, span_y, depth = grad_ref.shape[1:]
    lines = planes * span_y
    units = one_ref.shape[0]
    i = pl.program_id(0)

    @pl.when(i == 0)
    def _():
        stage[...] = jnp.zeros_like(stage)
        acc_mid[...] = jnp.zeros_like(acc_mid)
        acc_in[...] = jnp.zeros_like(acc_in)
        acc_out[...] = jnp.zeros_like(acc_out)
        acc_b[...] = jnp.zeros_like(acc_b)
        out = jnp.concatenate([w_out[...].astype(F32), jnp.zeros((13, units), F32)], 0)
        w_out_t[...] = out.T.astype(BF16)
        w_mid_t[...] = w_mid[...].astype(F32).T.astype(BF16)

    for k in range(planes):
        for c in range(3):
            stage[pl.ds(16 * span_y * k + c, span_y, stride=16), :] = grad_ref[c, k].astype(F32)
    grad = jnp.concatenate([stage[16 * y : 16 * y + 16, :].astype(BF16) for y in range(lines)], 1)
    bias = stage[0:8, :]
    for y in range(1, lines):
        bias = bias + stage[16 * y : 16 * y + 8, :]
    acc_b[...] += bias
    hidden_one, hidden_two = one_ref[...], two_ref[...]
    acc_out[...] += dot_nt(grad, hidden_two)
    two_value = hidden_two.astype(F32)
    delta_two = (dot(w_out_t[...], grad) * (1.0 - two_value * two_value)).astype(BF16)
    ones = jnp.ones((16, hidden_one.shape[1]), BF16)
    acc_mid[...] += dot_nt(jnp.concatenate([hidden_one, ones], 0), delta_two)
    one_value = hidden_one.astype(F32)
    delta_one = (dot(w_mid_t[...], delta_two) * (1.0 - one_value * one_value)).astype(BF16)
    acc_in[...] += dot_nt(feat_ref[...], delta_one)

    @pl.when(i == pl.num_programs(0) - 1)
    def _():
        sum_ref[...] = jnp.zeros_like(sum_ref)
        sum_ref[0:units, :] = acc_mid[0:units, :]
        sum_ref[units : units + 13, :] = acc_in[0:13, :]
        sum_ref[units + 13 : units + 14, :] = acc_mid[units : units + 1, :]
        sum_ref[units + 14 : units + 17, :] = acc_out[0:3, :]
        lane = lax.broadcasted_iota(jnp.int32, (1, units), 1)
        row = jnp.where(lane == 3, jnp.sum(cost_ref[...]), 0.0)
        for c in range(3):
            row = row + jnp.where(lane == c, jnp.sum(acc_b[c : c + 1, :]), 0.0)
        sum_ref[units + 17 : units + 18, :] = row


def finish_kernel(spot_of, entry_total, cell_total, *refs):
    n = len(refs) - 8
    pieces = refs[:n]
    loss_ref, in_ref, b_in_ref, mid_ref, b_mid_ref, out_ref, b_out_ref, whole = refs[n:]
    units = mid_ref.shape[0]
    feats = in_ref.shape[0]
    size = pieces[0].shape[0]
    for ref, spot in zip(pieces, spot_of()):
        whole[pl.ds(pl.multiple_of(spot * size, 8), size), :] = ref[...]
    mid = whole[0:units, :]
    small = whole[units : units + 32, :]
    row = lax.broadcasted_iota(jnp.int32, small.shape, 0)
    lane = lax.broadcasted_iota(jnp.int32, small.shape, 1)
    counted = (row < feats + 5) | ((row == feats + 5) & (lane < 3))
    squares = jnp.sum(mid * mid) + jnp.sum(jnp.where(counted, small * small, 0.0))
    scale = jnp.full((1, 1), 1.0, F32) / jnp.sqrt(jnp.full((1, 1), 1.0, F32) * squares / entry_total + EPSILON_RMS)
    small = small * scale
    mid_ref[...] = (mid * scale).T
    in_ref[...] = small[0:feats]
    b_in_ref[...] = small[feats : feats + 1]
    b_mid_ref[...] = small[feats + 1 : feats + 2]
    out_ref[...] = small[feats + 2 : feats + 5]
    b_out_ref[...] = small[feats + 5 : feats + 6, 0:3]
    loss_ref[...] = whole[units + feats + 5 : units + feats + 6, 3:4] / cell_total


def is_power(count):
    return count & (count - 1) == 0


def partner(index, step, count):
    return index ^ step if is_power(count) else (index + step) % count


def pair_list(count, offset):
    pairs = []
    for low in range(offset, count - 1, 2):
        pairs += [(low, low + 1), (low + 1, low)]
    return pairs


def face_plan(n_x, n_y):
    plan = []
    for dim, count in ((0, n_x), (1, n_y)):
        if count > 1:
            plan.append((dim, 0))
        if count > 2:
            plan.append((dim, 1))
    return tuple(plan)


def swap(values, axis, step):
    count = lax.axis_size(axis)
    return lax.ppermute(values, axis, [(i, partner(i, step, count)) for i in range(count)])


def swap_both(values, step_x, step_y):
    n_x, n_y = lax.axis_size("gx"), lax.axis_size("gy")
    pairs = [
        (i * n_y + j, partner(i, step_x, n_x) * n_y + partner(j, step_y, n_y)) for i in range(n_x) for j in range(n_y)
    ]
    return lax.ppermute(values, ("gx", "gy"), pairs)


def gather_doubling(values, order):
    held = {(0, 0): values}
    for axis, bit in order:
        for (sx, sy), block in list(held.items()):
            key = (sx ^ bit, sy) if axis == "gx" else (sx, sy ^ bit)
            held[key] = swap(block, axis, bit)
    return held


def bits_of(axis, count):
    return [(axis, 1 << k) for k in reversed(range(count.bit_length() - 1))]


def on_device(
    velocity,
    target,
    weight_in,
    bias_in,
    weight_mid,
    bias_mid,
    weight_out,
    bias_out,
    thrust_coef,
    tile_cells,
    tile_turbine,
    tile_weight,
):
    v, t = velocity[0], target[0]
    _, span_x, span_y, depth = v.shape
    units, feats = weight_in.shape
    cells = span_x * span_y * depth
    turbines = thrust_coef.shape[0]
    n_case, n_x, n_y = lax.axis_size("case"), lax.axis_size("gx"), lax.axis_size("gy")
    ix, iy = lax.axis_index("gx"), lax.axis_index("gy")
    plan = face_plan(n_x, n_y)
    shape_of = jax.ShapeDtypeStruct

    start_kernel.plan = plan
    started = pl.pallas_call(
        start_kernel,
        name="start",
        out_shape=tuple(shape_of((6, span_y if d == 0 else span_x, depth), BF16) for d, _ in plan)
        + (shape_of((8, turbines), F32),),
        in_specs=[vspec(), sspec(), vspec(), vspec(), vspec()],
        out_specs=tuple(vspec() for _ in range(len(plan) + 1)),
        compiler_params=pltpu.CompilerParams(vmem_limit_bytes=LIMIT),
    )(tile_cells, tile_turbine, tile_weight, v, t)
    disk = started[-1]
    faces = []
    for face, (dim, parity) in zip(started[:-1], plan):
        axis, count = (("gx", n_x), ("gy", n_y))[dim]
        faces.append(lax.ppermute(face, axis, pair_list(count, parity)))
    if n_y > 1 and is_power(n_y) and is_power(n_x):
        disk = disk + swap(disk, "gy", 1)
        disks = [disk] + [
            swap_both(disk, a, b) for a in range(n_x) for b in range(0, n_y, 2) if (a, b) != (0, 0)
        ]
    else:
        disks = [swap_both(disk, a, b) for a in range(n_x) for b in range(n_y)]

    whole = lambda shape: pl.BlockSpec(shape, lambda i: (0,) * len(shape))
    planes = 2 if span_x % 2 == 0 else 1
    chunk = planes * span_y * depth
    face_shape = [f.shape for f in faces]
    hidden_one, hidden_two, features, closure = pl.pallas_call(
        functools.partial(forward_kernel, plan, len(faces)),
        name="closure_forward",
        grid=(span_x // planes,),
        out_shape=(
            shape_of((units, cells), BF16),
            shape_of((units, cells), BF16),
            shape_of((16, cells), BF16),
            shape_of((3, span_x, span_y, depth), F32),
        ),
        in_specs=[whole(s) for s in face_shape]
        + [
            whole(v.shape),
            whole((feats, units)),
            whole((1, units)),
            whole(weight_mid.shape),
            whole((1, units)),
            whole(weight_out.shape),
            sspec(),
        ],
        out_specs=(
            pl.BlockSpec((units, chunk), lambda i: (0, i)),
            pl.BlockSpec((units, chunk), lambda i: (0, i)),
            pl.BlockSpec((16, chunk), lambda i: (0, i)),
            pl.BlockSpec((3, planes, span_y, depth), lambda i: (0, i, 0, 0)),
        ),
        scratch_shapes=[
            VMEM((3, span_x + 2, span_y + 16, depth), F32),
            VMEM((16 * planes * span_y, depth), F32),
            VMEM((8 * planes * span_y, depth), F32),
            VMEM((units, 16), BF16),
            VMEM((units, 8), F32),
        ],
        compiler_params=pltpu.CompilerParams(vmem_limit_bytes=LIMIT),
    )(*faces, v, weight_in.T, bias_in.reshape(1, units), weight_mid, bias_mid.reshape(1, units), weight_out, bias_out)

    basis, modes = (jnp.asarray(a) for a in depth_basis(depth))
    message = shape_of((span_x + 2, span_y, depth), F32)
    prov, first, second = pl.pallas_call(
        functools.partial(provisional_kernel, plan, len(faces), len(disks)),
        name="provisional",
        out_shape=(shape_of(v.shape, BF16), message, message),
        in_specs=[sspec()] + [vspec() for _ in range(len(faces) + len(disks) + 7)],
        out_specs=(vspec(), vspec(), vspec()),
        scratch_shapes=[
            VMEM((3, span_x + 2, span_y + 16, depth), F32),
            VMEM((span_x * span_y, depth), F32),
            VMEM((3, span_x + 2, span_y + 16, depth), F32),
            VMEM(message.shape, F32),
            VMEM(message.shape, F32),
        ],
        compiler_params=pltpu.CompilerParams(vmem_limit_bytes=LIMIT),
    )(tile_turbine, *faces, *disks, tile_cells, tile_weight, thrust_coef.reshape(1, turbines), v, t, closure, basis)

    if is_power(n_x) and is_power(n_y):
        x_bits, y_bits = bits_of("gx", n_x), bits_of("gy", n_y)
        firsts = gather_doubling(first, x_bits + y_bits)
        seconds = gather_doubling(second, y_bits[:-1] + x_bits + y_bits[-1:])
    else:
        steps = [(a, b) for a in range(n_x) for b in range(n_y)]
        firsts = {s: swap_both(first, *s) for s in steps}
        seconds = {s: swap_both(second, *s) for s in steps}
    offsets = sorted(firsts)
    total_x, total_y = n_x * span_x, n_y * span_y
    new, force_field, cost = pl.pallas_call(
        functools.partial(solve_kernel, tuple(offsets), n_x, n_y),
        name="solve",
        out_shape=(shape_of(v.shape, BF16), shape_of(v.shape, BF16), shape_of((8, depth), F32)),
        in_specs=[vspec() for _ in range(2 * len(offsets) + 4)],
        out_specs=(vspec(), vspec(), vspec()),
        scratch_shapes=[
            VMEM((total_x + 2, total_y + 16, depth), F32),
            VMEM((total_x, total_y, depth), F32),
            VMEM((total_x, total_y, depth), F32),
            VMEM((total_x + 4, total_y + 16, depth), F32),
            VMEM((total_x + 4, total_y + 16, depth), F32),
            VMEM((3, span_x, span_y, depth), F32),
            VMEM((3, span_x * span_y, depth), F32),
            VMEM((total_x, total_y, depth), F32),
        ],
        compiler_params=pltpu.CompilerParams(vmem_limit_bytes=LIMIT),
    )(*[firsts[o] for o in offsets], *[seconds[o] for o in offsets], prov, t, basis, modes)

    n_pieces = n_x * n_y
    total_rows = -(-(units + 32) // (8 * n_pieces)) * 8 * n_pieces
    sums = pl.pallas_call(
        backward_kernel,
        name="closure_backward",
        grid=(span_x // planes,),
        out_shape=shape_of((total_rows, units), F32),
        in_specs=[
            pl.BlockSpec((3, planes, span_y, depth), lambda i: (0, i, 0, 0)),
            pl.BlockSpec((16, chunk), lambda i: (0, i)),
            pl.BlockSpec((units, chunk), lambda i: (0, i)),
            pl.BlockSpec((units, chunk), lambda i: (0, i)),
            whole(weight_out.shape),
            whole(weight_mid.shape),
            whole((8, depth)),
        ],
        out_specs=whole((total_rows, units)),
        scratch_shapes=[
            VMEM((16 * planes * span_y, depth), F32),
            VMEM((units + 16, units), F32),
            VMEM((16, units), F32),
            VMEM((16, units), F32),
            VMEM((8, depth), F32),
            VMEM((units, 16), BF16),
            VMEM((units, units), BF16),
        ],
        compiler_params=pltpu.CompilerParams(vmem_limit_bytes=LIMIT),
    )(force_field, features, hidden_one, hidden_two, weight_out, weight_mid, cost)

    if n_y > 1 and is_power(n_x) and is_power(n_y) and is_power(n_case):
        group = n_pieces // 2
        size = total_rows // n_pieces
        sums = sums + swap(sums, "gy", 1)
        mine = lax.dynamic_slice_in_dim(sums, (iy & 1) * (group * size), group * size, 0)
        steps = [(a, b) for a in range(n_x) for b in range(0, n_y, 2)]
        spot = lambda a, b: (ix ^ a) * (n_y // 2) + ((iy ^ b) >> 1)
        cut = lambda s: lax.dynamic_slice_in_dim(mine, spot(*s) * size, size, 0)
        piece = cut((0, 0))
        for s in steps[1:]:
            piece = piece + swap_both(cut(s), *s)
        for _, bit in reversed(bits_of("case", n_case)):
            piece = piece + swap(piece, "case", bit)
        here = [piece] + [swap_both(piece, *s) for s in steps[1:]]
        there = [swap(p, "gy", 1) for p in here]
        pieces = here + there

        def spot_of():
            jx, jy = lax.axis_index("gx"), lax.axis_index("gy")
            base = [(jx ^ a) * (n_y // 2) + ((jy ^ b) >> 1) for a, b in steps]
            return [(jy & 1) * group + k for k in base] + [(1 - (jy & 1)) * group + k for k in base]

    else:
        pieces = [lax.psum(sums, ("case", "gx", "gy"))]
        spot_of = lambda: [0]

    entry_total = units * feats + units + units * units + units + 3 * units + 3
    cell_total = 3 * cells * n_case * n_x * n_y
    loss, s_in, sb_in, s_mid, sb_mid, s_out, sb_out = pl.pallas_call(
        functools.partial(finish_kernel, spot_of, entry_total, cell_total),
        name="finish",
        out_shape=(
            shape_of((1, 1), F32),
            shape_of((feats, units), F32),
            shape_of((1, units), F32),
            shape_of((units, units), F32),
            shape_of((1, units), F32),
            shape_of((3, units), F32),
            shape_of((1, 3), F32),
        ),
        in_specs=[vspec() for _ in pieces],
        out_specs=tuple(vspec() for _ in range(7)),
        scratch_shapes=[VMEM((total_rows, units), F32)],
        compiler_params=pltpu.CompilerParams(vmem_limit_bytes=LIMIT),
    )(*pieces)
    return (
        new[None],
        loss.reshape(()),
        s_in.T,
        sb_in.reshape(units),
        s_mid,
        sb_mid.reshape(units),
        s_out,
        sb_out.reshape(3),
        force_field[None],
    )


def solution(mesh):
    placed = (
        P("case", None, "gx", "gy", None),
        P("case", None, "gx", "gy", None),
        P(),
        P(),
        P(),
        P(),
        P(),
        P(),
        P(),
        P(("gx", "gy"), None),
        P(("gx", "gy")),
        P(("gx", "gy"), None),
    )
    field = P("case", None, "gx", "gy", None)
    return jax.shard_map(
        on_device,
        mesh=mesh,
        in_specs=placed,
        out_specs=(field, P(), P(), P(), P(), P(), P(), P(), field),
        check_vma=False,
    )
```

```python
import functools

import jax
import jax.numpy as jnp
import numpy as np
from jax import lax
from jax.experimental import pallas as pl
from jax.experimental.pallas import tpu as pltpu
from jax.sharding import PartitionSpec as P


ITERS = 20
INFLOW = 1.0
STEP_DT = 0.4
VISCOSITY = 0.1
EPSILON_RMS = 1e-06

F32 = jnp.float32
BF16 = jnp.bfloat16
VMEM = pltpu.VMEM
MIB = 1024 * 1024
LIMIT = 58 * MIB
ROOM = 60 * 1024 * 1024


def parity_of(dim):
    return lax.axis_index(("gx", "gy")[dim]) & 1


def vspec():
    return pl.BlockSpec(memory_space=pltpu.VMEM)


def sspec():
    return pl.BlockSpec(memory_space=pltpu.SMEM)


def dot(a, b):
    return lax.dot_general(a, b, (((1,), (0,)), ((), ())), preferred_element_type=F32)


def dot_nt(a, b):
    return lax.dot_general(a, b, (((1,), (1,)), ((), ())), preferred_element_type=F32)


def dot_full(a, b):
    return lax.dot_general(
        a, b, (((1,), (0,)), ((), ())), precision=lax.Precision.HIGHEST, preferred_element_type=F32
    )


def depth_basis(depth):
    mode = np.arange(1, depth + 1, dtype=np.float64)
    basis = np.sqrt(2.0 / (depth + 1)) * np.sin(np.pi * np.outer(mode, mode) / (depth + 1))
    slope = 0.5 * (np.eye(depth, k=-1) - np.eye(depth, k=1))
    matrices = np.stack([basis, basis @ slope, basis @ slope @ slope @ basis])
    return matrices.astype(np.float32), (2.0 * np.cos(np.pi * mode / (depth + 1))).astype(np.float32)[None]


def lane_shifts(values, step=1):
    depth = values.shape[-1]
    axis = values.ndim - 1
    lane = lax.broadcasted_iota(jnp.int32, values.shape, axis)
    up = jnp.where(lane < depth - step, pltpu.roll(values, depth - step, axis), 0.0)
    down = jnp.where(lane >= step, pltpu.roll(values, step, axis), 0.0)
    return up, down


def start_kernel(cells_ref, turbine_ref, weight_ref, v_ref, t_ref, *outs):
    n_x_sends = (len(outs) - 1) // 2 if False else None
    del n_x_sends
    face_refs, disk_ref = outs[:-1], outs[-1]
    span_x, span_y, depth = v_ref.shape[1:]
    for ref, (dim, high_parity) in zip(face_refs, start_kernel.plan):
        take_high = parity_of(dim) == high_parity
        for part, source in enumerate((v_ref, t_ref)):
            for c in range(3):
                if dim == 0:
                    high, low = source[c, span_x - 1], source[c, 0]
                    ref[3 * part + c] = jnp.where(take_high, high.astype(F32), low.astype(F32)).astype(BF16)
                else:
                    for x in range(span_x):
                        plane = source[c, x].astype(F32)
                        row = jnp.where(take_high, plane[span_y - 1 : span_y], plane[0:1])
                        ref[3 * part + c, x : x + 1, :] = row.astype(BF16)
    rows = span_x * span_y
    tiles, width = cells_ref.shape
    stream = v_ref[0].astype(F32).reshape(rows, depth).T.astype(BF16)
    pick = []
    for r in range(tiles):
        cell_row = cells_ref[r : r + 1, :] // depth
        spot = lax.broadcasted_iota(jnp.int32, (rows, width), 0)
        pick.append((spot == cell_row).astype(F32).astype(BF16))
    found = dot(stream, jnp.concatenate(pick, 1))
    turbines = disk_ref.shape[1]
    lane = lax.broadcasted_iota(jnp.int32, (1, turbines), 1)
    total = jnp.zeros((1, turbines), F32)
    area = jnp.zeros((1, turbines), F32)
    spot = lax.broadcasted_iota(jnp.int32, (depth, width), 0)
    for r in range(tiles):
        cell_lane = cells_ref[r : r + 1, :] % depth
        values = jnp.sum(jnp.where(spot == cell_lane, found[:, r * width : (r + 1) * width], 0.0), 0, keepdims=True)
        weight = weight_ref[r : r + 1, :]
        weighted = jnp.sum(weight * (values + INFLOW), 1, keepdims=True)
        summed = jnp.sum(weight, 1, keepdims=True)
        mine = lane == turbine_ref[r]
        total = total + jnp.where(mine, weighted, 0.0)
        area = area + jnp.where(mine, summed, 0.0)
    disk_ref[...] = jnp.zeros_like(disk_ref)
    disk_ref[0:1, :] = total
    disk_ref[1:2, :] = area


def fill_padded(pad, source, first, faces, plan):
    span_x, span_y = source.shape[1], source.shape[2]
    depth = source.shape[3]
    zero_plane = jnp.zeros((span_y, depth), F32)
    zero_rows = jnp.zeros((span_x, depth), F32)
    for c in range(3):
        for x in range(span_x):
            pad[c, 1 + x, 8 : 8 + span_y, :] = source[c, x].astype(F32)
        low = {0: zero_plane, 1: zero_rows}
        high = {0: zero_plane, 1: zero_rows}
        for ref, (dim, high_parity) in zip(faces, plan):
            got = ref[first + c].astype(F32)
            is_high = parity_of(dim) == high_parity
            high[dim] = jnp.where(is_high, got, high[dim])
            low[dim] = jnp.where(is_high, low[dim], got)
        pad[c, 0, 8 : 8 + span_y, :] = low[0]
        pad[c, 1 + span_x, 8 : 8 + span_y, :] = high[0]
        for x in range(span_x):
            pad[c, 1 + x, 7:8, :] = low[1][x : x + 1]
            pad[c, 1 + x, 8 + span_y : 9 + span_y, :] = high[1][x : x + 1]


def forward_kernel(plan, n_faces, *refs):
    faces = refs[:n_faces]
    (
        v_ref, w_in_t, b_in, w_mid, b_mid, w_out, b_out,
        one_ref, two_ref, feat_ref, closure_ref,
        pad, stage, stage_out, w_in, b_column, held,
    ) = refs[n_faces:]
    span_y, depth = v_ref.shape[2], v_ref.shape[3]
    planes = closure_ref.shape[1]
    lines = planes * span_y
    i = pl.program_id(0)

    def prepare(step):
        for k in range(planes):
            x = step * planes + k
            own = slice(8, 8 + span_y)

            def put(channel, value):
                stage[pl.ds(16 * span_y * k + channel, span_y, stride=16), :] = value

            for c in range(3):
                centre = pad[c, x + 1, own, :]
                put(c, 0.5 * (pad[c, x + 2, own, :] - pad[c, x, own, :]))
                put(3 + c, 0.5 * (pad[c, x + 1, 9 : 9 + span_y, :] - pad[c, x + 1, 7 : 7 + span_y, :]))
                up, down = lane_shifts(centre)
                put(6 + c, 0.5 * (up - down))
                put(9 + c, centre)
        held[...] = jnp.concatenate([stage[16 * y : 16 * y + 16, :].astype(BF16) for y in range(lines)], 1)

    def begin(k, carry):
        fill_padded(pad, v_ref, 0, faces, plan)
        channel = lax.broadcasted_iota(jnp.int32, stage.shape, 0) % 16
        stage[...] = jnp.where((channel >= 12) & (channel < 15), 1.0, 0.0)
        bias = b_in[...]
        high = bias.astype(BF16).astype(F32)
        rest = bias - high
        middle = rest.astype(BF16).astype(F32)
        rows = jnp.concatenate([w_in_t[...].astype(F32), high, middle, rest - middle, jnp.zeros_like(bias)], 0)
        w_in[...] = rows.T.astype(BF16)
        b_column[...] = jnp.broadcast_to(b_mid[...], (8, bias.shape[1])).T
        prepare(0)
        return carry

    lax.fori_loop(0, jnp.where(i == 0, 1, 0), begin, 0)

    features = held[...]
    feat_ref[...] = features
    prepare(jnp.minimum(i + 1, pl.num_programs(0) - 1))
    hidden_one = jnp.tanh(dot(w_in[...], features)).astype(BF16)
    one_ref[...] = hidden_one
    hidden_two = jnp.tanh(dot(w_mid[...], hidden_one) + b_column[:, 0:1]).astype(BF16)
    two_ref[...] = hidden_two
    out = dot(w_out[...], hidden_two)
    for y in range(lines):
        stage_out[8 * y : 8 * y + 3, :] = out[:, y * depth : (y + 1) * depth]
    for k in range(planes):
        for c in range(3):
            closure_ref[c, k] = stage_out[pl.ds(8 * span_y * k + c, span_y, stride=8), :] + b_out[c]


def provisional_kernel(plan, n_faces, n_disks, turbine_ref, *refs):
    faces = refs[:n_faces]
    disks = refs[n_faces : n_faces + n_disks]
    (cells_ref, weight_ref, coef_ref, v_ref, t_ref, closure_ref, basis_ref, prov_ref, first_out, second_out, pad, force, qpad, first_ref, second_ref) = refs[
        n_faces + n_disks :
    ]
    span_x, span_y, depth = v_ref.shape[1:]
    rows = span_x * span_y
    tiles, width = cells_ref.shape
    half = span_x // 2
    sums = disks[0][...]
    for extra in disks[1:]:
        sums = sums + extra[...]
    speed = sums[0:1, :] / jnp.maximum(sums[1:2, :], 1.0)
    thrust = -0.5 * coef_ref[...] * speed * jnp.abs(speed)
    lane = lax.broadcasted_iota(jnp.int32, thrust.shape, 1)
    spot_row = lax.broadcasted_iota(jnp.int32, (rows, width), 0)
    spot_lane = lax.broadcasted_iota(jnp.int32, (depth, width), 0)
    pick, spread = [], []
    for r in range(tiles):
        row_thrust = jnp.sum(jnp.where(lane == turbine_ref[r], thrust, 0.0), 1, keepdims=True)
        strength = weight_ref[r : r + 1, :] * row_thrust
        cell = cells_ref[r : r + 1, :]
        pick.append((spot_row == cell // depth).astype(F32).astype(BF16))
        spread.append(jnp.where(spot_lane == cell % depth, strength, 0.0))
    pick = jnp.concatenate(pick, 1)
    spread = jnp.concatenate(spread, 1)
    hi = spread.astype(BF16)
    rest = spread - hi.astype(F32)
    mid = rest.astype(BF16)
    low = (rest - mid.astype(F32)).astype(BF16)
    force[...] = dot_nt(pick, hi) + (dot_nt(pick, mid) + dot_nt(pick, low))

    fill_padded(pad, t_ref, 3, faces, plan)
    for x in range(span_x):
        up, down = lane_shifts(pad[2, x + 1, 8 : 8 + span_y, :])
        value = (
            0.5 * (pad[0, x + 2, 8 : 8 + span_y, :] - pad[0, x, 8 : 8 + span_y, :])
            + 0.5 * (pad[1, x + 1, 9 : 9 + span_y, :] - pad[1, x + 1, 7 : 7 + span_y, :])
            + 0.5 * (up - down)
        )
        where_to = first_ref if x < half else second_ref
        where_to[half + x % half] = value

    fill_padded(pad, v_ref, 0, faces, plan)
    qpad[...] = jnp.zeros_like(qpad)
    for x in range(span_x):
        centre = [pad[c, x + 1, 8 : 8 + span_y, :] for c in range(3)]
        for c in range(3):
            xp, xm = pad[c, x + 2, 8 : 8 + span_y, :], pad[c, x, 8 : 8 + span_y, :]
            yp, ym = pad[c, x + 1, 9 : 9 + span_y, :], pad[c, x + 1, 7 : 7 + span_y, :]
            zp, zm = lane_shifts(centre[c])
            laplace = (xp + xm) + yp + ym + zp + zm - 6.0 * centre[c]
            advect = (
                (centre[0] + INFLOW) * (0.5 * (xp - xm)) + centre[1] * (0.5 * (yp - ym)) + centre[2] * (0.5 * (zp - zm))
            )
            tendency = VISCOSITY * laplace - advect + closure_ref[c, x]
            if c == 0:
                tendency = tendency + force[x * span_y : (x + 1) * span_y, :]
            value = (centre[c] + STEP_DT * tendency).astype(BF16)
            prov_ref[c, x] = value
            qpad[c, 1 + x, 8 : 8 + span_y, :] = value.astype(F32)
    for x in range(span_x):
        up, down = lane_shifts(qpad[2, x + 1, 8 : 8 + span_y, :])
        value = (
            0.5 * (qpad[0, x + 2, 8 : 8 + span_y, :] - qpad[0, x, 8 : 8 + span_y, :])
            + 0.5 * (qpad[1, x + 1, 9 : 9 + span_y, :] - qpad[1, x + 1, 7 : 7 + span_y, :])
            + 0.5 * (up - down)
        )
        where_to = first_ref if x < half else second_ref
        where_to[x % half] = value
        second_ref[2 * half, x : x + 1, :] = 0.5 * qpad[1, 1 + x, 8:9, :]
        second_ref[2 * half + 1, x : x + 1, :] = -0.5 * qpad[1, 1 + x, 7 + span_y : 8 + span_y, :]
    first_ref[2 * half] = 0.5 * qpad[0, 1, 8 : 8 + span_y, :]
    first_ref[2 * half + 1] = -0.5 * qpad[0, span_x, 8 : 8 + span_y, :]
    for scratch, out in ((first_ref, first_out), (second_ref, second_out)):
        out[...] = dot_full(scratch[...].reshape(-1, depth), basis_ref[0]).reshape(out.shape)


def solve_kernel(offsets, n_x, n_y, *refs):
    n = len(offsets)
    firsts, seconds = refs[:n], refs[n : 2 * n]
    q_ref, t_ref, basis_ref, modes_ref, new_ref, grad_ref, cost_ref, div, div_t, source, pa, pb, seed, moved, twice = refs[2 * n :]
    span_x, span_y, depth = q_ref.shape[1:]
    total_x, total_y = source.shape[0], source.shape[1]
    half = span_x // 2
    rows = slice(8, 8 + total_y)
    ix, iy = lax.axis_index("gx"), lax.axis_index("gy")

    for buffer in (pa, pb):
        for edge in (buffer.at[0:2], buffer.at[total_x + 2 : total_x + 4], buffer.at[:, 0:8], buffer.at[:, 8 + total_y :]):
            edge[...] = jnp.zeros(edge.shape, F32)
    spots = []
    for mx, my in offsets:
        spots.append((partner(ix, mx, total_x // span_x) * span_x, pl.multiple_of(partner(iy, my, total_y // span_y) * span_y, span_y)))
    for k, (x0, y0) in enumerate(spots):
        for ref, base in ((firsts[k], 0), (seconds[k], half)):
            for x in range(half):
                div[x0 + base + x + 1, pl.ds(pl.multiple_of(y0 + 8, 8), span_y), :] = ref[x]
                div_t[x0 + base + x, pl.ds(y0, span_y), :] = ref[half + x]
    for k, (x0, y0) in enumerate(spots):
        own = pl.ds(pl.multiple_of(y0 + 8, 8), span_y)
        div[x0, own, :] = div[x0, own, :] + firsts[k][2 * half]
        div[x0 + span_x + 1, own, :] = div[x0 + span_x + 1, own, :] + firsts[k][2 * half + 1]
        for x in range(span_x):
            below = pl.ds(y0 + 7, 1)
            above = pl.ds(y0 + 8 + span_y, 1)
            div[x0 + x + 1, below, :] = div[x0 + x + 1, below, :] + seconds[k][2 * half, x : x + 1, :]
            div[x0 + x + 1, above, :] = div[x0 + x + 1, above, :] + seconds[k][2 * half + 1, x : x + 1, :]

    unit = 1.0 / (6.0 * STEP_DT)

    def first_source(x, carry):
        value = div[x + 1, rows, :] * unit
        source[x] = value
        pa[x + 2, rows, :] = -value
        return carry

    lax.fori_loop(0, total_x, first_source, 0, unroll=4)

    def sweep(src, dst, x_start, x_count, y_start, y_count):
        own = pl.ds(y_start + 8, y_count)
        mode = modes_ref[...]
        group = x_count if x_count <= 32 else 32

        def planes(i, carry):
            base = x_start + i * group
            loaded = {}

            def plane(k):
                if k not in loaded:
                    loaded[k] = src[base + k, own, :]
                return loaded[k]

            for k in range(group):
                centre = plane(k + 2)
                across = plane(k + 1) + plane(k + 3)
                beside = src[base + k + 2, pl.ds(y_start + 9, y_count), :] + src[base + k + 2, pl.ds(y_start + 7, y_count), :]
                around = (across + beside) + mode * centre
                dst[base + k + 2, own, :] = around * (1.0 / 6.0) - source[base + k, pl.ds(y_start, y_count), :]
                loaded.pop(k + 1)
            return carry

        if x_count == group:
            planes(0, 0)
        else:
            lax.fori_loop(0, x_count // group, planes, 0)

    def run(stages, start=0):
        buffers, now = (pa, pb), start
        for window, count in stages:

            def two(k, carry, now=now, window=window):
                sweep(buffers[now], buffers[1 - now], *window)
                sweep(buffers[1 - now], buffers[now], *window)
                return carry

            if count // 2:
                lax.fori_loop(0, count // 2, two, 0)
            if count % 2:
                sweep(buffers[now], buffers[1 - now], *window)
                now = 1 - now
        return buffers[now]

    whole = (0, total_x, 0, total_y)

    def windows():
        stages = []
        left = ITERS - 1
        for k in range(left):
            margin = -(-(left - k) // 8) * 8
            x_count = min(total_x, span_x + margin * min(n_x - 1, 2))
            y_count = min(total_y, span_y + margin * min(n_y - 1, 2))
            key = (margin, x_count, y_count)
            if stages and (stages[-1][0][1:] == key[1:]):
                stages[-1][1] += 1
            else:
                stages.append([key, 1])
        result = []
        for (margin, x_count, y_count), count in stages:
            x_start = 0 if x_count == total_x else jnp.clip(ix * span_x - margin, 0, total_x - x_count)
            y_start = 0
            if y_count != total_y:
                y_start = pl.multiple_of(jnp.clip(iy * span_y - margin, 0, total_y - y_count), 8)
            result.append(((x_start, x_count, y_start, y_count), count))
        return result

    def correction(p):
        y0 = pl.multiple_of(iy * span_y, 8)
        own = pl.ds(pl.multiple_of(y0 + 8, 8), span_y)
        for x in range(span_x):
            at = ix * span_x + x + 2
            wide = p[at, pl.ds(y0, span_y + 16), :]
            lines = slice(x * span_y, (x + 1) * span_y)
            moved[0, lines, :] = (0.5 * STEP_DT) * (p[at + 1, own, :] - p[at - 1, own, :])
            moved[1, lines, :] = (0.5 * STEP_DT) * (wide[9 : 9 + span_y] - wide[7 : 7 + span_y])
            moved[2, lines, :] = STEP_DT * wide[8 : 8 + span_y]
        for c in range(3):
            moved[c] = dot_full(moved[c], basis_ref[0 if c < 2 else 1])

    p = run([(whole, ITERS - 1)])
    cost = jnp.zeros((span_y, depth), F32)
    correction(p)
    for x in range(span_x):
        for c in range(3):
            updated = q_ref[c, x].astype(F32) - moved[c, x * span_y : (x + 1) * span_y, :]
            new_ref[c, x] = updated.astype(BF16)
            mismatch = updated - t_ref[c, x].astype(F32)
            cost = cost + mismatch * mismatch
            seed[c, x] = 2.0 * mismatch
    cost_ref[...] = cost[0:8] + sum((cost[k : k + 8] for k in range(8, span_y, 8)), jnp.zeros((8, depth), F32))

    other = pa if p is pb else pb
    together = 8

    def vertical(i, carry):
        some = pl.ds(i * together, together)
        values = p[pl.ds(i * together + 2, together), rows, :].reshape(-1, depth)
        twice[some] = dot_full(values, basis_ref[2]).reshape(together, total_y, depth)
        return carry

    lax.fori_loop(0, total_x // together, vertical, 0)

    def second_source(x, carry):
        centre = p[x + 2, rows, :]
        to_high = jnp.where(x + 1 < total_x, 0.25, 0.0)
        to_low = jnp.where(x > 0, 0.25, 0.0)
        wide = to_high * (p[x + 4, rows, :] - centre) - to_low * (centre - p[x, rows, :])
        row = lax.broadcasted_iota(jnp.int32, centre.shape, 0)
        wide = wide + 0.25 * (
            jnp.where(row < total_y - 1, p[x + 2, 10 : 10 + total_y, :] - centre, 0.0)
            - jnp.where(row > 0, centre - p[x + 2, 6 : 6 + total_y, :], 0.0)
        )
        wide = wide + twice[x]
        value = (2.0 * unit) * (div[x + 1, rows, :] - STEP_DT * wide - div_t[x])
        source[x] = value
        other[x + 2, rows, :] = -value
        return carry

    lax.fori_loop(0, total_x, second_source, 0, unroll=4)
    p = run(windows(), start=0 if p is pb else 1)
    correction(p)
    for x in range(span_x):
        for c in range(3):
            grad_ref[c, x] = (STEP_DT * (seed[c, x] - moved[c, x * span_y : (x + 1) * span_y, :])).astype(BF16)


def backward_kernel(n_sums, grad_ref, feat_ref, one_ref, two_ref, w_out, w_mid, cost_ref, *refs):
    sum_refs = refs[:n_sums]
    stage, acc_mid, acc_in, acc_out, acc_b, w_out_t, w_mid_t, whole = refs[n_sums:]
    planes, span_y, depth = grad_ref.shape[1:]
    lines = planes * span_y
    units = one_ref.shape[0]
    i = pl.program_id(0)

    @pl.when(i == 0)
    def _():
        stage[...] = jnp.zeros_like(stage)
        acc_mid[...] = jnp.zeros_like(acc_mid)
        acc_in[...] = jnp.zeros_like(acc_in)
        acc_out[...] = jnp.zeros_like(acc_out)
        acc_b[...] = jnp.zeros_like(acc_b)
        out = jnp.concatenate([w_out[...].astype(F32), jnp.zeros((13, units), F32)], 0)
        w_out_t[...] = out.T.astype(BF16)
        w_mid_t[...] = w_mid[...].astype(F32).T.astype(BF16)

    for k in range(planes):
        for c in range(3):
            stage[pl.ds(16 * span_y * k + c, span_y, stride=16), :] = grad_ref[c, k].astype(F32)
    grad = jnp.concatenate([stage[16 * y : 16 * y + 16, :].astype(BF16) for y in range(lines)], 1)
    bias = stage[0:8, :]
    for y in range(1, lines):
        bias = bias + stage[16 * y : 16 * y + 8, :]
    acc_b[...] += bias
    hidden_one, hidden_two = one_ref[...], two_ref[...]
    two_value = hidden_two.astype(F32)
    delta_two = (dot(w_out_t[...], grad) * (1.0 - two_value * two_value)).astype(BF16)
    ones = jnp.ones((16, hidden_one.shape[1]), BF16)
    acc_mid[...] += dot_nt(jnp.concatenate([hidden_one, ones], 0), delta_two)
    one_value = hidden_one.astype(F32)
    delta_one = (dot(w_mid_t[...], delta_two) * (1.0 - one_value * one_value)).astype(BF16)
    acc_out[...] += dot_nt(grad, hidden_two)
    acc_in[...] += dot_nt(feat_ref[...], delta_one)

    @pl.when(i == pl.num_programs(0) - 1)
    def _():
        whole[...] = jnp.zeros_like(whole)
        whole[0:units, :] = acc_mid[0:units, :]
        whole[units : units + 13, :] = acc_in[0:13, :]
        whole[units + 13 : units + 14, :] = acc_mid[units : units + 1, :]
        whole[units + 14 : units + 17, :] = acc_out[0:3, :]
        lane = lax.broadcasted_iota(jnp.int32, (1, units), 1)
        row = jnp.where(lane == 3, jnp.sum(cost_ref[...]), 0.0)
        for c in range(3):
            row = row + jnp.where(lane == c, jnp.sum(acc_b[c : c + 1, :]), 0.0)
        whole[units + 17 : units + 18, :] = row
        if len(sum_refs) == 1:
            sum_refs[0][...] = whole[...]
        else:
            size = sum_refs[0].shape[0]
            mine = parity_of(1)
            sum_refs[0][...] = whole[pl.ds(pl.multiple_of(mine * size, 8), size), :]
            sum_refs[1][...] = whole[pl.ds(pl.multiple_of((1 - mine) * size, 8), size), :]


def finish_kernel(spot_of, entry_total, cell_total, *refs):
    n = len(refs) - 8
    pieces = refs[:n]
    loss_ref, in_ref, b_in_ref, mid_ref, b_mid_ref, out_ref, b_out_ref, whole = refs[n:]
    units = mid_ref.shape[0]
    feats = in_ref.shape[0]
    size = pieces[0].shape[0]
    for ref, spot in zip(pieces, spot_of()):
        whole[pl.ds(pl.multiple_of(spot * size, 8), size), :] = ref[...]
    mid = whole[0:units, :]
    small = whole[units : units + 32, :]
    row = lax.broadcasted_iota(jnp.int32, small.shape, 0)
    lane = lax.broadcasted_iota(jnp.int32, small.shape, 1)
    counted = (row < feats + 5) | ((row == feats + 5) & (lane < 3))
    squares = jnp.sum(mid * mid) + jnp.sum(jnp.where(counted, small * small, 0.0))
    scale = jnp.full((1, 1), 1.0, F32) / jnp.sqrt(jnp.full((1, 1), 1.0, F32) * squares / entry_total + EPSILON_RMS)
    small = small * scale
    mid_ref[...] = (mid * scale).T
    in_ref[...] = small[0:feats]
    b_in_ref[...] = small[feats : feats + 1]
    b_mid_ref[...] = small[feats + 1 : feats + 2]
    out_ref[...] = small[feats + 2 : feats + 5]
    b_out_ref[...] = small[feats + 5 : feats + 6, 0:3]
    loss_ref[...] = whole[units + feats + 5 : units + feats + 6, 3:4] / cell_total


def is_power(count):
    return count & (count - 1) == 0


def partner(index, step, count):
    return index ^ step if is_power(count) else (index + step) % count


def pair_list(count, offset):
    pairs = []
    for low in range(offset, count - 1, 2):
        pairs += [(low, low + 1), (low + 1, low)]
    return pairs


def face_plan(n_x, n_y):
    plan = []
    for dim, count in ((0, n_x), (1, n_y)):
        if count > 1:
            plan.append((dim, 0))
        if count > 2:
            plan.append((dim, 1))
    return tuple(plan)


def swap(values, axis, step):
    count = lax.axis_size(axis)
    return lax.ppermute(values, axis, [(i, partner(i, step, count)) for i in range(count)])


def swap_both(values, step_x, step_y):
    n_x, n_y = lax.axis_size("gx"), lax.axis_size("gy")
    pairs = [
        (i * n_y + j, partner(i, step_x, n_x) * n_y + partner(j, step_y, n_y)) for i in range(n_x) for j in range(n_y)
    ]
    return lax.ppermute(values, ("gx", "gy"), pairs)


def gather_doubling(values, order):
    held = {(0, 0): values}
    for axis, bit in order:
        for (sx, sy), block in list(held.items()):
            key = (sx ^ bit, sy) if axis == "gx" else (sx, sy ^ bit)
            held[key] = swap(block, axis, bit)
    return held


def bits_of(axis, count):
    return [(axis, 1 << k) for k in reversed(range(count.bit_length() - 1))]


def on_device(
    velocity,
    target,
    weight_in,
    bias_in,
    weight_mid,
    bias_mid,
    weight_out,
    bias_out,
    thrust_coef,
    tile_cells,
    tile_turbine,
    tile_weight,
):
    stay = lambda x: pltpu.with_memory_space_constraint(x, pltpu.HBM)
    v, t = stay(velocity[0]), stay(target[0])
    _, span_x, span_y, depth = v.shape
    units, feats = weight_in.shape
    cells = span_x * span_y * depth
    turbines = thrust_coef.shape[0]
    n_case, n_x, n_y = lax.axis_size("case"), lax.axis_size("gx"), lax.axis_size("gy")
    ix, iy = lax.axis_index("gx"), lax.axis_index("gy")
    plan = face_plan(n_x, n_y)
    shape_of = jax.ShapeDtypeStruct

    start_kernel.plan = plan
    started = pl.pallas_call(
        start_kernel,
        name="start",
        out_shape=tuple(shape_of((6, span_y if d == 0 else span_x, depth), BF16) for d, _ in plan)
        + (shape_of((8, turbines), F32),),
        in_specs=[vspec(), sspec(), vspec(), vspec(), vspec()],
        out_specs=tuple(vspec() for _ in range(len(plan) + 1)),
        compiler_params=pltpu.CompilerParams(vmem_limit_bytes=LIMIT),
    )(tile_cells, tile_turbine, tile_weight, v, t)
    disk = started[-1]
    faces = []
    for face, (dim, parity) in zip(started[:-1], plan):
        axis, count = (("gx", n_x), ("gy", n_y))[dim]
        faces.append(lax.ppermute(face, axis, pair_list(count, parity)))
    if n_y > 1 and is_power(n_y) and is_power(n_x):
        disk = disk + swap(disk, "gy", 1)
        disks = [disk] + [
            swap_both(disk, a, b) for a in range(n_x) for b in range(0, n_y, 2) if (a, b) != (0, 0)
        ]
    else:
        disks = [swap_both(disk, a, b) for a in range(n_x) for b in range(n_y)]

    total_x, total_y = n_x * span_x, n_y * span_y
    solve_need = 4 * depth * ((total_x + 4) * (total_y + 16) * 6 + 8 * span_x * span_y) + 6 * MIB
    shared = max(ROOM - 4 * units * cells - MIB // 4, solve_need)
    whole = lambda shape: pl.BlockSpec(shape, lambda i: (0,) * len(shape))
    planes = 2
    chunk = planes * span_y * depth
    face_shape = [f.shape for f in faces]
    hidden_one, hidden_two, features, closure = pl.pallas_call(
        functools.partial(forward_kernel, plan, len(faces)),
        name="closure_forward",
        grid=(span_x // planes,),
        out_shape=(
            shape_of((units, cells), BF16),
            shape_of((units, cells), BF16),
            shape_of((16, cells), BF16),
            shape_of((3, span_x, span_y, depth), F32),
        ),
        in_specs=[whole(s) for s in face_shape]
        + [
            whole(v.shape),
            whole((feats, units)),
            whole((1, units)),
            whole(weight_mid.shape),
            whole((1, units)),
            whole(weight_out.shape),
            sspec(),
        ],
        out_specs=(
            pl.BlockSpec((units, chunk), lambda i: (0, i)),
            pl.BlockSpec((units, chunk), lambda i: (0, i)),
            pl.BlockSpec((16, chunk), lambda i: (0, i)),
            pl.BlockSpec((3, planes, span_y, depth), lambda i: (0, i, 0, 0)),
        ),
        scratch_shapes=[
            VMEM((3, span_x + 2, span_y + 16, depth), F32),
            VMEM((16 * planes * span_y, depth), F32),
            VMEM((8 * planes * span_y, depth), F32),
            VMEM((units, 16), BF16),
            VMEM((units, 8), F32),
            VMEM((16, chunk), BF16),
        ],
        compiler_params=pltpu.CompilerParams(vmem_limit_bytes=shared),
    )(*faces, v, stay(weight_in.T), stay(bias_in.reshape(1, units)), stay(weight_mid), stay(bias_mid.reshape(1, units)), stay(weight_out), stay(bias_out))

    basis, modes = (jnp.asarray(a) for a in depth_basis(depth))
    message = shape_of((span_x + 2, span_y, depth), F32)
    prov, first, second = pl.pallas_call(
        functools.partial(provisional_kernel, plan, len(faces), len(disks)),
        name="provisional",
        out_shape=(shape_of(v.shape, BF16), message, message),
        in_specs=[sspec()] + [vspec() for _ in range(len(faces) + len(disks) + 7)],
        out_specs=(vspec(), vspec(), vspec()),
        scratch_shapes=[
            VMEM((3, span_x + 2, span_y + 16, depth), F32),
            VMEM((span_x * span_y, depth), F32),
            VMEM((3, span_x + 2, span_y + 16, depth), F32),
            VMEM(message.shape, F32),
            VMEM(message.shape, F32),
        ],
        compiler_params=pltpu.CompilerParams(vmem_limit_bytes=shared),
    )(stay(tile_turbine), *faces, *disks, stay(tile_cells), stay(tile_weight), stay(thrust_coef.reshape(1, turbines)), v, t, closure, stay(basis))

    if is_power(n_x) and is_power(n_y):
        x_bits, y_bits = bits_of("gx", n_x), bits_of("gy", n_y)
        firsts = gather_doubling(first, x_bits + y_bits)
        seconds = gather_doubling(second, y_bits[:-1] + x_bits + y_bits[-1:])
    else:
        steps = [(a, b) for a in range(n_x) for b in range(n_y)]
        firsts = {s: swap_both(first, *s) for s in steps}
        seconds = {s: swap_both(second, *s) for s in steps}
    offsets = sorted(firsts)
    total_x, total_y = n_x * span_x, n_y * span_y
    new, force_field, cost = pl.pallas_call(
        functools.partial(solve_kernel, tuple(offsets), n_x, n_y),
        name="solve",
        out_shape=(shape_of(v.shape, BF16), shape_of(v.shape, BF16), shape_of((8, depth), F32)),
        in_specs=[vspec() for _ in range(2 * len(offsets) + 4)],
        out_specs=(vspec(), vspec(), vspec()),
        scratch_shapes=[
            VMEM((total_x + 2, total_y + 16, depth), F32),
            VMEM((total_x, total_y, depth), F32),
            VMEM((total_x, total_y, depth), F32),
            VMEM((total_x + 4, total_y + 16, depth), F32),
            VMEM((total_x + 4, total_y + 16, depth), F32),
            VMEM((3, span_x, span_y, depth), F32),
            VMEM((3, span_x * span_y, depth), F32),
            VMEM((total_x, total_y, depth), F32),
        ],
        compiler_params=pltpu.CompilerParams(vmem_limit_bytes=shared),
    )(*[firsts[o] for o in offsets], *[seconds[o] for o in offsets], prov, t, stay(basis), stay(modes))

    n_pieces = n_x * n_y
    total_rows = -(-(units + 32) // (8 * n_pieces)) * 8 * n_pieces
    paired = n_y > 1 and is_power(n_x) and is_power(n_y) and is_power(n_case)
    n_sums = 2 if paired else 1
    planes = 1
    chunk = planes * span_y * depth
    sums = pl.pallas_call(
        functools.partial(backward_kernel, n_sums),
        name="closure_backward",
        grid=(span_x // planes,),
        out_shape=(shape_of((total_rows // n_sums, units), F32),) * n_sums,
        in_specs=[
            pl.BlockSpec((3, planes, span_y, depth), lambda i: (0, i, 0, 0)),
            pl.BlockSpec((16, chunk), lambda i: (0, i)),
            pl.BlockSpec((units, chunk), lambda i: (0, i)),
            pl.BlockSpec((units, chunk), lambda i: (0, i)),
            whole(weight_out.shape),
            whole(weight_mid.shape),
            whole((8, depth)),
        ],
        out_specs=(whole((total_rows // n_sums, units)),) * n_sums,
        scratch_shapes=[
            VMEM((16 * planes * span_y, depth), F32),
            VMEM((units + 16, units), F32),
            VMEM((16, units), F32),
            VMEM((16, units), F32),
            VMEM((8, depth), F32),
            VMEM((units, 16), BF16),
            VMEM((units, units), BF16),
            VMEM((total_rows, units), F32),
        ],
        compiler_params=pltpu.CompilerParams(vmem_limit_bytes=shared),
    )(stay(force_field), features, hidden_one, hidden_two, stay(weight_out), stay(weight_mid), cost)

    if paired:
        group = n_pieces // 2
        size = total_rows // n_pieces
        mine = sums[0] + swap(sums[1], "gy", 1)
        steps = [(a, b) for a in range(n_x) for b in range(0, n_y, 2)]
        spot = lambda a, b: (ix ^ a) * (n_y // 2) + ((iy ^ b) >> 1)
        cut = lambda s: lax.dynamic_slice_in_dim(mine, spot(*s) * size, size, 0)
        piece = cut((0, 0))
        for s in steps[1:]:
            piece = piece + swap_both(cut(s), *s)
        for _, bit in reversed(bits_of("case", n_case)):
            piece = piece + swap(piece, "case", bit)
        here = [piece] + [swap_both(piece, *s) for s in steps[1:]]
        there = [swap(p, "gy", 1) for p in here]
        pieces = here + there

        def spot_of():
            jx, jy = lax.axis_index("gx"), lax.axis_index("gy")
            base = [(jx ^ a) * (n_y // 2) + ((jy ^ b) >> 1) for a, b in steps]
            return [(jy & 1) * group + k for k in base] + [(1 - (jy & 1)) * group + k for k in base]

    else:
        pieces = [lax.psum(sums[0], ("case", "gx", "gy"))]
        spot_of = lambda: [0]

    entry_total = units * feats + units + units * units + units + 3 * units + 3
    cell_total = 3 * cells * n_case * n_x * n_y
    loss, s_in, sb_in, s_mid, sb_mid, s_out, sb_out = pl.pallas_call(
        functools.partial(finish_kernel, spot_of, entry_total, cell_total),
        name="finish",
        out_shape=(
            shape_of((1, 1), F32),
            shape_of((feats, units), F32),
            shape_of((1, units), F32),
            shape_of((units, units), F32),
            shape_of((1, units), F32),
            shape_of((3, units), F32),
            shape_of((1, 3), F32),
        ),
        in_specs=[vspec() for _ in pieces],
        out_specs=tuple(vspec() for _ in range(7)),
        scratch_shapes=[VMEM((total_rows, units), F32)],
        compiler_params=pltpu.CompilerParams(vmem_limit_bytes=LIMIT),
    )(*pieces)
    return (
        new[None],
        loss.reshape(()),
        s_in.T,
        sb_in.reshape(units),
        s_mid,
        sb_mid.reshape(units),
        s_out,
        sb_out.reshape(3),
        force_field[None],
    )


def solution(mesh):
    placed = (
        P("case", None, "gx", "gy", None),
        P("case", None, "gx", "gy", None),
        P(),
        P(),
        P(),
        P(),
        P(),
        P(),
        P(),
        P(("gx", "gy"), None),
        P(("gx", "gy")),
        P(("gx", "gy"), None),
    )
    field = P("case", None, "gx", "gy", None)
    return jax.shard_map(
        on_device,
        mesh=mesh,
        in_specs=placed,
        out_specs=(field, P(), P(), P(), P(), P(), P(), P(), field),
        check_vma=False,
    )
```

```python
import functools

import jax
import jax.numpy as jnp
import numpy as np
from jax import lax
from jax.experimental import pallas as pl
from jax.experimental.pallas import tpu as pltpu
from jax.sharding import PartitionSpec as P


ITERS = 20
INFLOW = 1.0
STEP_DT = 0.4
VISCOSITY = 0.1
EPSILON_RMS = 1e-06

F32 = jnp.float32
BF16 = jnp.bfloat16
VMEM = pltpu.VMEM
MIB = 1024 * 1024
LIMIT = 58 * MIB
ROOM = 60 * 1024 * 1024


def parity_of(dim):
    return lax.axis_index(("gx", "gy")[dim]) & 1


def vspec():
    return pl.BlockSpec(memory_space=pltpu.VMEM)


def sspec():
    return pl.BlockSpec(memory_space=pltpu.SMEM)


def dot(a, b):
    return lax.dot_general(a, b, (((1,), (0,)), ((), ())), preferred_element_type=F32)


def dot_nt(a, b):
    return lax.dot_general(a, b, (((1,), (1,)), ((), ())), preferred_element_type=F32)


def dot_full(a, b):
    return lax.dot_general(
        a, b, (((1,), (0,)), ((), ())), precision=lax.Precision.HIGHEST, preferred_element_type=F32
    )


def depth_basis(depth):
    mode = np.arange(1, depth + 1, dtype=np.float64)
    basis = np.sqrt(2.0 / (depth + 1)) * np.sin(np.pi * np.outer(mode, mode) / (depth + 1))
    slope = 0.5 * (np.eye(depth, k=-1) - np.eye(depth, k=1))
    matrices = np.stack([basis, basis @ slope, basis @ slope @ slope @ basis])
    return matrices.astype(np.float32), (2.0 * np.cos(np.pi * mode / (depth + 1))).astype(np.float32)[None]


def lane_shifts(values, step=1):
    depth = values.shape[-1]
    axis = values.ndim - 1
    lane = lax.broadcasted_iota(jnp.int32, values.shape, axis)
    up = jnp.where(lane < depth - step, pltpu.roll(values, depth - step, axis), 0.0)
    down = jnp.where(lane >= step, pltpu.roll(values, step, axis), 0.0)
    return up, down


def start_kernel(cells_ref, turbine_ref, weight_ref, v_ref, t_ref, *outs):
    n_x_sends = (len(outs) - 1) // 2 if False else None
    del n_x_sends
    face_refs, disk_ref = outs[:-1], outs[-1]
    span_x, span_y, depth = v_ref.shape[1:]
    for ref, (dim, high_parity) in zip(face_refs, start_kernel.plan):
        take_high = parity_of(dim) == high_parity
        for part, source in enumerate((v_ref, t_ref)):
            for c in range(3):
                if dim == 0:
                    high, low = source[c, span_x - 1], source[c, 0]
                    ref[3 * part + c] = jnp.where(take_high, high.astype(F32), low.astype(F32)).astype(BF16)
                else:
                    for x in range(span_x):
                        plane = source[c, x].astype(F32)
                        row = jnp.where(take_high, plane[span_y - 1 : span_y], plane[0:1])
                        ref[3 * part + c, x : x + 1, :] = row.astype(BF16)
    rows = span_x * span_y
    tiles, width = cells_ref.shape
    stream = v_ref[0].astype(F32).reshape(rows, depth).T.astype(BF16)
    pick = []
    for r in range(tiles):
        cell_row = cells_ref[r : r + 1, :] // depth
        spot = lax.broadcasted_iota(jnp.int32, (rows, width), 0)
        pick.append((spot == cell_row).astype(F32).astype(BF16))
    found = dot(stream, jnp.concatenate(pick, 1))
    turbines = disk_ref.shape[1]
    lane = lax.broadcasted_iota(jnp.int32, (1, turbines), 1)
    total = jnp.zeros((1, turbines), F32)
    area = jnp.zeros((1, turbines), F32)
    spot = lax.broadcasted_iota(jnp.int32, (depth, width), 0)
    for r in range(tiles):
        cell_lane = cells_ref[r : r + 1, :] % depth
        values = jnp.sum(jnp.where(spot == cell_lane, found[:, r * width : (r + 1) * width], 0.0), 0, keepdims=True)
        weight = weight_ref[r : r + 1, :]
        weighted = jnp.sum(weight * (values + INFLOW), 1, keepdims=True)
        summed = jnp.sum(weight, 1, keepdims=True)
        mine = lane == turbine_ref[r]
        total = total + jnp.where(mine, weighted, 0.0)
        area = area + jnp.where(mine, summed, 0.0)
    disk_ref[...] = jnp.zeros_like(disk_ref)
    disk_ref[0:1, :] = total
    disk_ref[1:2, :] = area


def fill_padded(pad, source, first, faces, plan):
    span_x, span_y = source.shape[1], source.shape[2]
    depth = source.shape[3]
    zero_plane = jnp.zeros((span_y, depth), F32)
    zero_rows = jnp.zeros((span_x, depth), F32)
    for c in range(3):
        for x in range(span_x):
            pad[c, 1 + x, 8 : 8 + span_y, :] = source[c, x].astype(F32)
        low = {0: zero_plane, 1: zero_rows}
        high = {0: zero_plane, 1: zero_rows}
        for ref, (dim, high_parity) in zip(faces, plan):
            got = ref[first + c].astype(F32)
            is_high = parity_of(dim) == high_parity
            high[dim] = jnp.where(is_high, got, high[dim])
            low[dim] = jnp.where(is_high, low[dim], got)
        pad[c, 0, 8 : 8 + span_y, :] = low[0]
        pad[c, 1 + span_x, 8 : 8 + span_y, :] = high[0]
        for x in range(span_x):
            pad[c, 1 + x, 7:8, :] = low[1][x : x + 1]
            pad[c, 1 + x, 8 + span_y : 9 + span_y, :] = high[1][x : x + 1]


def forward_kernel(plan, n_faces, *refs):
    faces = refs[:n_faces]
    (
        v_ref, w_in_t, b_in, w_mid, b_mid, w_out, b_out,
        one_ref, two_ref, feat_ref, closure_ref,
        pad, stage, stage_out, w_in, b_column, held,
    ) = refs[n_faces:]
    span_y, depth = v_ref.shape[2], v_ref.shape[3]
    planes = closure_ref.shape[1]
    lines = planes * span_y
    i = pl.program_id(0)

    def prepare(step):
        for k in range(planes):
            x = step * planes + k
            own = slice(8, 8 + span_y)

            def put(channel, value):
                stage[pl.ds(16 * span_y * k + channel, span_y, stride=16), :] = value

            for c in range(3):
                centre = pad[c, x + 1, own, :]
                put(c, 0.5 * (pad[c, x + 2, own, :] - pad[c, x, own, :]))
                put(3 + c, 0.5 * (pad[c, x + 1, 9 : 9 + span_y, :] - pad[c, x + 1, 7 : 7 + span_y, :]))
                up, down = lane_shifts(centre)
                put(6 + c, 0.5 * (up - down))
                put(9 + c, centre)
        held[...] = jnp.concatenate([stage[16 * y : 16 * y + 16, :].astype(BF16) for y in range(lines)], 1)

    def begin(k, carry):
        fill_padded(pad, v_ref, 0, faces, plan)
        channel = lax.broadcasted_iota(jnp.int32, stage.shape, 0) % 16
        stage[...] = jnp.where((channel >= 12) & (channel < 15), 1.0, 0.0)
        bias = b_in[...]
        high = bias.astype(BF16).astype(F32)
        rest = bias - high
        middle = rest.astype(BF16).astype(F32)
        rows = jnp.concatenate([w_in_t[...].astype(F32), high, middle, rest - middle, jnp.zeros_like(bias)], 0)
        w_in[...] = rows.T.astype(BF16)
        b_column[...] = jnp.broadcast_to(b_mid[...], (8, bias.shape[1])).T
        prepare(0)
        return carry

    lax.fori_loop(0, jnp.where(i == 0, 1, 0), begin, 0)

    features = held[...]
    feat_ref[...] = features
    prepare(jnp.minimum(i + 1, pl.num_programs(0) - 1))
    hidden_one = jnp.tanh(dot(w_in[...], features)).astype(BF16)
    one_ref[...] = hidden_one
    hidden_two = jnp.tanh(dot(w_mid[...], hidden_one) + b_column[:, 0:1]).astype(BF16)
    two_ref[...] = hidden_two
    out = dot(w_out[...], hidden_two)
    for y in range(lines):
        stage_out[8 * y : 8 * y + 3, :] = out[:, y * depth : (y + 1) * depth]
    for k in range(planes):
        for c in range(3):
            closure_ref[c, k] = stage_out[pl.ds(8 * span_y * k + c, span_y, stride=8), :] + b_out[c]


def provisional_kernel(plan, n_faces, n_disks, turbine_ref, *refs):
    faces = refs[:n_faces]
    disks = refs[n_faces : n_faces + n_disks]
    (cells_ref, weight_ref, coef_ref, v_ref, t_ref, closure_ref, basis_ref, prov_ref, first_out, second_out, pad, force, qpad, first_ref, second_ref) = refs[
        n_faces + n_disks :
    ]
    span_x, span_y, depth = v_ref.shape[1:]
    rows = span_x * span_y
    tiles, width = cells_ref.shape
    half = span_x // 2
    sums = disks[0][...]
    for extra in disks[1:]:
        sums = sums + extra[...]
    speed = sums[0:1, :] / jnp.maximum(sums[1:2, :], 1.0)
    thrust = -0.5 * coef_ref[...] * speed * jnp.abs(speed)
    lane = lax.broadcasted_iota(jnp.int32, thrust.shape, 1)
    spot_row = lax.broadcasted_iota(jnp.int32, (rows, width), 0)
    spot_lane = lax.broadcasted_iota(jnp.int32, (depth, width), 0)
    pick, spread = [], []
    for r in range(tiles):
        row_thrust = jnp.sum(jnp.where(lane == turbine_ref[r], thrust, 0.0), 1, keepdims=True)
        strength = weight_ref[r : r + 1, :] * row_thrust
        cell = cells_ref[r : r + 1, :]
        pick.append((spot_row == cell // depth).astype(F32).astype(BF16))
        spread.append(jnp.where(spot_lane == cell % depth, strength, 0.0))
    pick = jnp.concatenate(pick, 1)
    spread = jnp.concatenate(spread, 1)
    hi = spread.astype(BF16)
    rest = spread - hi.astype(F32)
    mid = rest.astype(BF16)
    low = (rest - mid.astype(F32)).astype(BF16)
    force[...] = dot_nt(pick, hi) + (dot_nt(pick, mid) + dot_nt(pick, low))

    fill_padded(pad, t_ref, 3, faces, plan)
    for x in range(span_x):
        up, down = lane_shifts(pad[2, x + 1, 8 : 8 + span_y, :])
        value = (
            0.5 * (pad[0, x + 2, 8 : 8 + span_y, :] - pad[0, x, 8 : 8 + span_y, :])
            + 0.5 * (pad[1, x + 1, 9 : 9 + span_y, :] - pad[1, x + 1, 7 : 7 + span_y, :])
            + 0.5 * (up - down)
        )
        where_to = first_ref if x < half else second_ref
        where_to[half + x % half] = value

    fill_padded(pad, v_ref, 0, faces, plan)
    qpad[...] = jnp.zeros_like(qpad)
    for x in range(span_x):
        centre = [pad[c, x + 1, 8 : 8 + span_y, :] for c in range(3)]
        for c in range(3):
            xp, xm = pad[c, x + 2, 8 : 8 + span_y, :], pad[c, x, 8 : 8 + span_y, :]
            yp, ym = pad[c, x + 1, 9 : 9 + span_y, :], pad[c, x + 1, 7 : 7 + span_y, :]
            zp, zm = lane_shifts(centre[c])
            laplace = (xp + xm) + yp + ym + zp + zm - 6.0 * centre[c]
            advect = (
                (centre[0] + INFLOW) * (0.5 * (xp - xm)) + centre[1] * (0.5 * (yp - ym)) + centre[2] * (0.5 * (zp - zm))
            )
            tendency = VISCOSITY * laplace - advect + closure_ref[c, x]
            if c == 0:
                tendency = tendency + force[x * span_y : (x + 1) * span_y, :]
            value = (centre[c] + STEP_DT * tendency).astype(BF16)
            prov_ref[c, x] = value
            qpad[c, 1 + x, 8 : 8 + span_y, :] = value.astype(F32)
    for x in range(span_x):
        up, down = lane_shifts(qpad[2, x + 1, 8 : 8 + span_y, :])
        value = (
            0.5 * (qpad[0, x + 2, 8 : 8 + span_y, :] - qpad[0, x, 8 : 8 + span_y, :])
            + 0.5 * (qpad[1, x + 1, 9 : 9 + span_y, :] - qpad[1, x + 1, 7 : 7 + span_y, :])
            + 0.5 * (up - down)
        )
        where_to = first_ref if x < half else second_ref
        where_to[x % half] = value
        second_ref[2 * half, x : x + 1, :] = 0.5 * qpad[1, 1 + x, 8:9, :]
        second_ref[2 * half + 1, x : x + 1, :] = -0.5 * qpad[1, 1 + x, 7 + span_y : 8 + span_y, :]
    first_ref[2 * half] = 0.5 * qpad[0, 1, 8 : 8 + span_y, :]
    first_ref[2 * half + 1] = -0.5 * qpad[0, span_x, 8 : 8 + span_y, :]
    for scratch, out in ((first_ref, first_out), (second_ref, second_out)):
        out[...] = dot_full(scratch[...].reshape(-1, depth), basis_ref[0]).reshape(out.shape)


def solve_kernel(offsets, n_x, n_y, *refs):
    n = len(offsets)
    firsts, seconds = refs[:n], refs[n : 2 * n]
    q_ref, t_ref, basis_ref, modes_ref, new_ref, grad_ref, cost_ref, div, div_t, source, pa, pb, seed, moved, twice = refs[2 * n :]
    span_x, span_y, depth = q_ref.shape[1:]
    total_x, total_y = source.shape[0], source.shape[1]
    half = span_x // 2
    rows = slice(8, 8 + total_y)
    ix, iy = lax.axis_index("gx"), lax.axis_index("gy")

    for buffer in (pa, pb):
        for edge in (buffer.at[0:2], buffer.at[total_x + 2 : total_x + 4], buffer.at[:, 0:8], buffer.at[:, 8 + total_y :]):
            edge[...] = jnp.zeros(edge.shape, F32)
    spots = []
    for mx, my in offsets:
        spots.append((partner(ix, mx, total_x // span_x) * span_x, pl.multiple_of(partner(iy, my, total_y // span_y) * span_y, span_y)))
    for k, (x0, y0) in enumerate(spots):
        for ref, base in ((firsts[k], 0), (seconds[k], half)):
            for x in range(half):
                div[x0 + base + x + 1, pl.ds(pl.multiple_of(y0 + 8, 8), span_y), :] = ref[x]
                div_t[x0 + base + x, pl.ds(y0, span_y), :] = ref[half + x]
    for k, (x0, y0) in enumerate(spots):
        own = pl.ds(pl.multiple_of(y0 + 8, 8), span_y)
        div[x0, own, :] = div[x0, own, :] + firsts[k][2 * half]
        div[x0 + span_x + 1, own, :] = div[x0 + span_x + 1, own, :] + firsts[k][2 * half + 1]
        for x in range(span_x):
            below = pl.ds(y0 + 7, 1)
            above = pl.ds(y0 + 8 + span_y, 1)
            div[x0 + x + 1, below, :] = div[x0 + x + 1, below, :] + seconds[k][2 * half, x : x + 1, :]
            div[x0 + x + 1, above, :] = div[x0 + x + 1, above, :] + seconds[k][2 * half + 1, x : x + 1, :]

    unit = 1.0 / (6.0 * STEP_DT)

    def first_source(x, carry):
        value = div[x + 1, rows, :] * unit
        source[x] = value
        pa[x + 2, rows, :] = -value
        return carry

    lax.fori_loop(0, total_x, first_source, 0, unroll=4)

    def sweep(src, dst, x_start, x_count, y_start, y_count):
        own = pl.ds(y_start + 8, y_count)
        mode = modes_ref[...]
        group = x_count if x_count <= 32 else 32

        def planes(i, carry):
            base = x_start + i * group
            loaded = {}

            def plane(k):
                if k not in loaded:
                    loaded[k] = src[base + k, own, :]
                return loaded[k]

            for k in range(group):
                centre = plane(k + 2)
                across = plane(k + 1) + plane(k + 3)
                beside = src[base + k + 2, pl.ds(y_start + 9, y_count), :] + src[base + k + 2, pl.ds(y_start + 7, y_count), :]
                around = (across + beside) + mode * centre
                dst[base + k + 2, own, :] = around * (1.0 / 6.0) - source[base + k, pl.ds(y_start, y_count), :]
                loaded.pop(k + 1)
            return carry

        if x_count == group:
            planes(0, 0)
        else:
            lax.fori_loop(0, x_count // group, planes, 0)

    def run(stages, start=0):
        buffers, now = (pa, pb), start
        for window, count in stages:

            def two(k, carry, now=now, window=window):
                sweep(buffers[now], buffers[1 - now], *window)
                sweep(buffers[1 - now], buffers[now], *window)
                return carry

            if count // 2:
                lax.fori_loop(0, count // 2, two, 0)
            if count % 2:
                sweep(buffers[now], buffers[1 - now], *window)
                now = 1 - now
        return buffers[now]

    whole = (0, total_x, 0, total_y)

    def windows():
        stages = []
        left = ITERS - 1
        for k in range(left):
            margin = -(-(left - k) // 8) * 8
            x_count = min(total_x, span_x + margin * min(n_x - 1, 2))
            y_count = min(total_y, span_y + margin * min(n_y - 1, 2))
            key = (margin, x_count, y_count)
            if stages and (stages[-1][0][1:] == key[1:]):
                stages[-1][1] += 1
            else:
                stages.append([key, 1])
        result = []
        for (margin, x_count, y_count), count in stages:
            x_start = 0 if x_count == total_x else jnp.clip(ix * span_x - margin, 0, total_x - x_count)
            y_start = 0
            if y_count != total_y:
                y_start = pl.multiple_of(jnp.clip(iy * span_y - margin, 0, total_y - y_count), 8)
            result.append(((x_start, x_count, y_start, y_count), count))
        return result

    def correction(p):
        y0 = pl.multiple_of(iy * span_y, 8)
        own = pl.ds(pl.multiple_of(y0 + 8, 8), span_y)
        for x in range(span_x):
            at = ix * span_x + x + 2
            wide = p[at, pl.ds(y0, span_y + 16), :]
            lines = slice(x * span_y, (x + 1) * span_y)
            moved[0, lines, :] = (0.5 * STEP_DT) * (p[at + 1, own, :] - p[at - 1, own, :])
            moved[1, lines, :] = (0.5 * STEP_DT) * (wide[9 : 9 + span_y] - wide[7 : 7 + span_y])
            moved[2, lines, :] = STEP_DT * wide[8 : 8 + span_y]
        for c in range(3):
            moved[c] = dot_full(moved[c], basis_ref[0 if c < 2 else 1])

    p = run([(whole, ITERS - 1)])
    cost = jnp.zeros((span_y, depth), F32)
    correction(p)
    for x in range(span_x):
        for c in range(3):
            updated = q_ref[c, x].astype(F32) - moved[c, x * span_y : (x + 1) * span_y, :]
            new_ref[c, x] = updated.astype(BF16)
            mismatch = updated - t_ref[c, x].astype(F32)
            cost = cost + mismatch * mismatch
            seed[c, x] = 2.0 * mismatch
    cost_ref[...] = cost[0:8] + sum((cost[k : k + 8] for k in range(8, span_y, 8)), jnp.zeros((8, depth), F32))

    other = pa if p is pb else pb
    together = 8

    def vertical(i, carry):
        some = pl.ds(i * together, together)
        values = p[pl.ds(i * together + 2, together), rows, :].reshape(-1, depth)
        twice[some] = dot_full(values, basis_ref[2]).reshape(together, total_y, depth)
        return carry

    lax.fori_loop(0, total_x // together, vertical, 0)

    def second_source(x, carry):
        centre = p[x + 2, rows, :]
        to_high = jnp.where(x + 1 < total_x, 0.25, 0.0)
        to_low = jnp.where(x > 0, 0.25, 0.0)
        wide = to_high * (p[x + 4, rows, :] - centre) - to_low * (centre - p[x, rows, :])
        row = lax.broadcasted_iota(jnp.int32, centre.shape, 0)
        wide = wide + 0.25 * (
            jnp.where(row < total_y - 1, p[x + 2, 10 : 10 + total_y, :] - centre, 0.0)
            - jnp.where(row > 0, centre - p[x + 2, 6 : 6 + total_y, :], 0.0)
        )
        wide = wide + twice[x]
        value = (2.0 * unit) * (div[x + 1, rows, :] - STEP_DT * wide - div_t[x])
        source[x] = value
        other[x + 2, rows, :] = -value
        return carry

    lax.fori_loop(0, total_x, second_source, 0, unroll=4)
    p = run(windows(), start=0 if p is pb else 1)
    correction(p)
    for x in range(span_x):
        for c in range(3):
            grad_ref[c, x] = (STEP_DT * (seed[c, x] - moved[c, x * span_y : (x + 1) * span_y, :])).astype(BF16)


def backward_kernel(n_sums, grad_ref, feat_ref, one_ref, two_ref, w_out, w_mid, cost_ref, *refs):
    sum_refs = refs[:n_sums]
    stage, acc_mid, acc_in, acc_out, acc_b, w_out_t, w_mid_t, whole = refs[n_sums:]
    planes, span_y, depth = grad_ref.shape[1:]
    lines = planes * span_y
    units = one_ref.shape[0]
    i = pl.program_id(0)

    @pl.when(i == 0)
    def _():
        stage[...] = jnp.zeros_like(stage)
        acc_mid[...] = jnp.zeros_like(acc_mid)
        acc_in[...] = jnp.zeros_like(acc_in)
        acc_out[...] = jnp.zeros_like(acc_out)
        acc_b[...] = jnp.zeros_like(acc_b)
        out = jnp.concatenate([w_out[...].astype(F32), jnp.zeros((13, units), F32)], 0)
        w_out_t[...] = out.T.astype(BF16)
        w_mid_t[...] = w_mid[...].astype(F32).T.astype(BF16)

    for k in range(planes):
        for c in range(3):
            stage[pl.ds(16 * span_y * k + c, span_y, stride=16), :] = grad_ref[c, k].astype(F32)
    grad = jnp.concatenate([stage[16 * y : 16 * y + 16, :].astype(BF16) for y in range(lines)], 1)
    bias = stage[0:8, :]
    for y in range(1, lines):
        bias = bias + stage[16 * y : 16 * y + 8, :]
    acc_b[...] += bias
    hidden_one, hidden_two = one_ref[...], two_ref[...]
    two_value = hidden_two.astype(F32)
    delta_two = (dot(w_out_t[...], grad) * (1.0 - two_value * two_value)).astype(BF16)
    ones = jnp.ones((16, hidden_one.shape[1]), BF16)
    acc_mid[...] += dot_nt(jnp.concatenate([hidden_one, ones], 0), delta_two)
    one_value = hidden_one.astype(F32)
    delta_one = (dot(w_mid_t[...], delta_two) * (1.0 - one_value * one_value)).astype(BF16)
    acc_out[...] += dot_nt(grad, hidden_two)
    acc_in[...] += dot_nt(feat_ref[...], delta_one)

    @pl.when(i == pl.num_programs(0) - 1)
    def _():
        whole[...] = jnp.zeros_like(whole)
        whole[0:units, :] = acc_mid[0:units, :]
        whole[units : units + 13, :] = acc_in[0:13, :]
        whole[units + 13 : units + 14, :] = acc_mid[units : units + 1, :]
        whole[units + 14 : units + 17, :] = acc_out[0:3, :]
        lane = lax.broadcasted_iota(jnp.int32, (1, units), 1)
        row = jnp.where(lane == 3, jnp.sum(cost_ref[...]), 0.0)
        for c in range(3):
            row = row + jnp.where(lane == c, jnp.sum(acc_b[c : c + 1, :]), 0.0)
        whole[units + 17 : units + 18, :] = row
        if len(sum_refs) == 1:
            sum_refs[0][...] = whole[...]
        else:
            size = sum_refs[0].shape[0]
            mine = parity_of(1)
            sum_refs[0][...] = whole[pl.ds(pl.multiple_of(mine * size, 8), size), :]
            sum_refs[1][...] = whole[pl.ds(pl.multiple_of((1 - mine) * size, 8), size), :]


def finish_kernel(spot_of, entry_total, cell_total, *refs):
    n = len(refs) - 8
    pieces = refs[:n]
    loss_ref, in_ref, b_in_ref, mid_ref, b_mid_ref, out_ref, b_out_ref, whole = refs[n:]
    units = mid_ref.shape[0]
    feats = in_ref.shape[0]
    size = pieces[0].shape[0]
    for ref, spot in zip(pieces, spot_of()):
        whole[pl.ds(pl.multiple_of(spot * size, 8), size), :] = ref[...]
    mid = whole[0:units, :]
    small = whole[units : units + 32, :]
    row = lax.broadcasted_iota(jnp.int32, small.shape, 0)
    lane = lax.broadcasted_iota(jnp.int32, small.shape, 1)
    counted = (row < feats + 5) | ((row == feats + 5) & (lane < 3))
    squares = jnp.sum(mid * mid) + jnp.sum(jnp.where(counted, small * small, 0.0))
    scale = jnp.full((1, 1), 1.0, F32) / jnp.sqrt(jnp.full((1, 1), 1.0, F32) * squares / entry_total + EPSILON_RMS)
    small = small * scale
    mid_ref[...] = (mid * scale).T
    in_ref[...] = small[0:feats]
    b_in_ref[...] = small[feats : feats + 1]
    b_mid_ref[...] = small[feats + 1 : feats + 2]
    out_ref[...] = small[feats + 2 : feats + 5]
    b_out_ref[...] = small[feats + 5 : feats + 6, 0:3]
    loss_ref[...] = whole[units + feats + 5 : units + feats + 6, 3:4] / cell_total


def is_power(count):
    return count & (count - 1) == 0


def partner(index, step, count):
    return index ^ step if is_power(count) else (index + step) % count


def pair_list(count, offset):
    pairs = []
    for low in range(offset, count - 1, 2):
        pairs += [(low, low + 1), (low + 1, low)]
    return pairs


def face_plan(n_x, n_y):
    plan = []
    for dim, count in ((0, n_x), (1, n_y)):
        if count > 1:
            plan.append((dim, 0))
        if count > 2:
            plan.append((dim, 1))
    return tuple(plan)


def swap(values, axis, step):
    count = lax.axis_size(axis)
    return lax.ppermute(values, axis, [(i, partner(i, step, count)) for i in range(count)])


def swap_both(values, step_x, step_y):
    n_x, n_y = lax.axis_size("gx"), lax.axis_size("gy")
    pairs = [
        (i * n_y + j, partner(i, step_x, n_x) * n_y + partner(j, step_y, n_y)) for i in range(n_x) for j in range(n_y)
    ]
    return lax.ppermute(values, ("gx", "gy"), pairs)


def gather_doubling(values, order):
    held = {(0, 0): values}
    for axis, bit in order:
        for (sx, sy), block in list(held.items()):
            key = (sx ^ bit, sy) if axis == "gx" else (sx, sy ^ bit)
            held[key] = swap(block, axis, bit)
    return held


def bits_of(axis, count):
    return [(axis, 1 << k) for k in reversed(range(count.bit_length() - 1))]


def on_device(
    velocity,
    target,
    weight_in,
    bias_in,
    weight_mid,
    bias_mid,
    weight_out,
    bias_out,
    thrust_coef,
    tile_cells,
    tile_turbine,
    tile_weight,
):
    stay = lambda x: pltpu.with_memory_space_constraint(x, pltpu.HBM)
    v, t = stay(velocity[0]), stay(target[0])
    _, span_x, span_y, depth = v.shape
    units, feats = weight_in.shape
    cells = span_x * span_y * depth
    turbines = thrust_coef.shape[0]
    n_case, n_x, n_y = lax.axis_size("case"), lax.axis_size("gx"), lax.axis_size("gy")
    ix, iy = lax.axis_index("gx"), lax.axis_index("gy")
    plan = face_plan(n_x, n_y)
    shape_of = jax.ShapeDtypeStruct

    start_kernel.plan = plan
    started = pl.pallas_call(
        start_kernel,
        name="start",
        out_shape=tuple(shape_of((6, span_y if d == 0 else span_x, depth), BF16) for d, _ in plan)
        + (shape_of((8, turbines), F32),),
        in_specs=[vspec(), sspec(), vspec(), vspec(), vspec()],
        out_specs=tuple(vspec() for _ in range(len(plan) + 1)),
        compiler_params=pltpu.CompilerParams(vmem_limit_bytes=24 * MIB),
    )(stay(tile_cells), stay(tile_turbine), stay(tile_weight), v, t)
    disk = started[-1]
    faces = []
    for face, (dim, parity) in zip(started[:-1], plan):
        axis, count = (("gx", n_x), ("gy", n_y))[dim]
        faces.append(lax.ppermute(face, axis, pair_list(count, parity)))
    if n_y > 1 and is_power(n_y) and is_power(n_x):
        disk = disk + swap(disk, "gy", 1)
        disks = [disk] + [
            swap_both(disk, a, b) for a in range(n_x) for b in range(0, n_y, 2) if (a, b) != (0, 0)
        ]
    else:
        disks = [swap_both(disk, a, b) for a in range(n_x) for b in range(n_y)]

    total_x, total_y = n_x * span_x, n_y * span_y
    solve_need = 4 * depth * ((total_x + 4) * (total_y + 16) * 6 + 8 * span_x * span_y) + 6 * MIB
    shared = max(ROOM - 4 * units * cells - MIB // 4, solve_need)
    whole = lambda shape: pl.BlockSpec(shape, lambda i: (0,) * len(shape))
    planes = 2
    chunk = planes * span_y * depth
    face_shape = [f.shape for f in faces]
    hidden_one, hidden_two, features, closure = pl.pallas_call(
        functools.partial(forward_kernel, plan, len(faces)),
        name="closure_forward",
        grid=(span_x // planes,),
        out_shape=(
            shape_of((units, cells), BF16),
            shape_of((units, cells), BF16),
            shape_of((16, cells), BF16),
            shape_of((3, span_x, span_y, depth), F32),
        ),
        in_specs=[whole(s) for s in face_shape]
        + [
            whole(v.shape),
            whole((feats, units)),
            whole((1, units)),
            whole(weight_mid.shape),
            whole((1, units)),
            whole(weight_out.shape),
            sspec(),
        ],
        out_specs=(
            pl.BlockSpec((units, chunk), lambda i: (0, i)),
            pl.BlockSpec((units, chunk), lambda i: (0, i)),
            pl.BlockSpec((16, chunk), lambda i: (0, i)),
            pl.BlockSpec((3, planes, span_y, depth), lambda i: (0, i, 0, 0)),
        ),
        scratch_shapes=[
            VMEM((3, span_x + 2, span_y + 16, depth), F32),
            VMEM((16 * planes * span_y, depth), F32),
            VMEM((8 * planes * span_y, depth), F32),
            VMEM((units, 16), BF16),
            VMEM((units, 8), F32),
            VMEM((16, chunk), BF16),
        ],
        compiler_params=pltpu.CompilerParams(vmem_limit_bytes=shared),
    )(*faces, v, stay(weight_in.T), stay(bias_in.reshape(1, units)), stay(weight_mid), stay(bias_mid.reshape(1, units)), stay(weight_out), stay(bias_out))

    basis, modes = (jnp.asarray(a) for a in depth_basis(depth))
    message = shape_of((span_x + 2, span_y, depth), F32)
    prov, first, second = pl.pallas_call(
        functools.partial(provisional_kernel, plan, len(faces), len(disks)),
        name="provisional",
        out_shape=(shape_of(v.shape, BF16), message, message),
        in_specs=[sspec()] + [vspec() for _ in range(len(faces) + len(disks) + 7)],
        out_specs=(vspec(), vspec(), vspec()),
        scratch_shapes=[
            VMEM((3, span_x + 2, span_y + 16, depth), F32),
            VMEM((span_x * span_y, depth), F32),
            VMEM((3, span_x + 2, span_y + 16, depth), F32),
            VMEM(message.shape, F32),
            VMEM(message.shape, F32),
        ],
        compiler_params=pltpu.CompilerParams(vmem_limit_bytes=shared),
    )(stay(tile_turbine), *faces, *disks, stay(tile_cells), stay(tile_weight), stay(thrust_coef.reshape(1, turbines)), v, t, closure, stay(basis))

    if is_power(n_x) and is_power(n_y):
        x_bits, y_bits = bits_of("gx", n_x), bits_of("gy", n_y)
        firsts = gather_doubling(first, x_bits + y_bits)
        seconds = gather_doubling(second, y_bits[:-1] + x_bits + y_bits[-1:])
    else:
        steps = [(a, b) for a in range(n_x) for b in range(n_y)]
        firsts = {s: swap_both(first, *s) for s in steps}
        seconds = {s: swap_both(second, *s) for s in steps}
    offsets = sorted(firsts)
    total_x, total_y = n_x * span_x, n_y * span_y
    new, force_field, cost = pl.pallas_call(
        functools.partial(solve_kernel, tuple(offsets), n_x, n_y),
        name="solve",
        out_shape=(shape_of(v.shape, BF16), shape_of(v.shape, BF16), shape_of((8, depth), F32)),
        in_specs=[vspec() for _ in range(2 * len(offsets) + 4)],
        out_specs=(vspec(), vspec(), vspec()),
        scratch_shapes=[
            VMEM((total_x + 2, total_y + 16, depth), F32),
            VMEM((total_x, total_y, depth), F32),
            VMEM((total_x, total_y, depth), F32),
            VMEM((total_x + 4, total_y + 16, depth), F32),
            VMEM((total_x + 4, total_y + 16, depth), F32),
            VMEM((3, span_x, span_y, depth), F32),
            VMEM((3, span_x * span_y, depth), F32),
            VMEM((total_x, total_y, depth), F32),
        ],
        compiler_params=pltpu.CompilerParams(vmem_limit_bytes=shared),
    )(*[firsts[o] for o in offsets], *[seconds[o] for o in offsets], prov, t, stay(basis), stay(modes))

    n_pieces = n_x * n_y
    total_rows = -(-(units + 32) // (8 * n_pieces)) * 8 * n_pieces
    paired = n_y > 1 and is_power(n_x) and is_power(n_y) and is_power(n_case)
    n_sums = 2 if paired else 1
    planes = 1
    chunk = planes * span_y * depth
    sums = pl.pallas_call(
        functools.partial(backward_kernel, n_sums),
        name="closure_backward",
        grid=(span_x // planes,),
        out_shape=(shape_of((total_rows // n_sums, units), F32),) * n_sums,
        in_specs=[
            pl.BlockSpec((3, planes, span_y, depth), lambda i: (0, i, 0, 0)),
            pl.BlockSpec((16, chunk), lambda i: (0, i)),
            pl.BlockSpec((units, chunk), lambda i: (0, i)),
            pl.BlockSpec((units, chunk), lambda i: (0, i)),
            whole(weight_out.shape),
            whole(weight_mid.shape),
            whole((8, depth)),
        ],
        out_specs=(whole((total_rows // n_sums, units)),) * n_sums,
        scratch_shapes=[
            VMEM((16 * planes * span_y, depth), F32),
            VMEM((units + 16, units), F32),
            VMEM((16, units), F32),
            VMEM((16, units), F32),
            VMEM((8, depth), F32),
            VMEM((units, 16), BF16),
            VMEM((units, units), BF16),
            VMEM((total_rows, units), F32),
        ],
        compiler_params=pltpu.CompilerParams(vmem_limit_bytes=shared),
    )(stay(force_field), features, hidden_one, hidden_two, stay(weight_out), stay(weight_mid), cost)

    if paired:
        group = n_pieces // 2
        size = total_rows // n_pieces
        mine = sums[0] + swap(sums[1], "gy", 1)
        steps = [(a, b) for a in range(n_x) for b in range(0, n_y, 2)]
        spot = lambda a, b: (ix ^ a) * (n_y // 2) + ((iy ^ b) >> 1)
        cut = lambda s: lax.dynamic_slice_in_dim(mine, spot(*s) * size, size, 0)
        piece = cut((0, 0))
        for s in steps[1:]:
            piece = piece + swap_both(cut(s), *s)
        for _, bit in reversed(bits_of("case", n_case)):
            piece = piece + swap(piece, "case", bit)
        here = [piece] + [swap_both(piece, *s) for s in steps[1:]]
        there = [swap(p, "gy", 1) for p in here]
        pieces = here + there

        def spot_of():
            jx, jy = lax.axis_index("gx"), lax.axis_index("gy")
            base = [(jx ^ a) * (n_y // 2) + ((jy ^ b) >> 1) for a, b in steps]
            return [(jy & 1) * group + k for k in base] + [(1 - (jy & 1)) * group + k for k in base]

    else:
        pieces = [lax.psum(sums[0], ("case", "gx", "gy"))]
        spot_of = lambda: [0]

    entry_total = units * feats + units + units * units + units + 3 * units + 3
    cell_total = 3 * cells * n_case * n_x * n_y
    loss, s_in, sb_in, s_mid, sb_mid, s_out, sb_out = pl.pallas_call(
        functools.partial(finish_kernel, spot_of, entry_total, cell_total),
        name="finish",
        out_shape=(
            shape_of((1, 1), F32),
            shape_of((feats, units), F32),
            shape_of((1, units), F32),
            shape_of((units, units), F32),
            shape_of((1, units), F32),
            shape_of((3, units), F32),
            shape_of((1, 3), F32),
        ),
        in_specs=[vspec() for _ in pieces],
        out_specs=tuple(vspec() for _ in range(7)),
        scratch_shapes=[VMEM((total_rows, units), F32)],
        compiler_params=pltpu.CompilerParams(vmem_limit_bytes=8 * MIB),
    )(*pieces)
    return (
        new[None],
        loss.reshape(()),
        s_in.T,
        sb_in.reshape(units),
        s_mid,
        sb_mid.reshape(units),
        s_out,
        sb_out.reshape(3),
        force_field[None],
    )


def solution(mesh):
    placed = (
        P("case", None, "gx", "gy", None),
        P("case", None, "gx", "gy", None),
        P(),
        P(),
        P(),
        P(),
        P(),
        P(),
        P(),
        P(("gx", "gy"), None),
        P(("gx", "gy")),
        P(("gx", "gy"), None),
    )
    field = P("case", None, "gx", "gy", None)
    return jax.shard_map(
        on_device,
        mesh=mesh,
        in_specs=placed,
        out_specs=(field, P(), P(), P(), P(), P(), P(), P(), field),
        check_vma=False,
    )
```
